32 devices in a mesh: blk: 8 (over y, x, core), split: 4 (over z).
Axes of the slice: x: 2, y: 2, z: 4, core: 2. Of those that a mesh axis runs over, the one named last changes fastest.
Arguments:
- ratings: bfloat16 [8, 6, 4, 80, 128, 128], P('blk', None, 'split'), may hold values from -6 to 6
- user_tile: int32 [8, 6, 4, 80], P('blk', None, 'split'), may hold values from 0 to 7
- item_tile: int32 [8, 6, 4, 80], P('blk', None, 'split'), may hold values from 0 to 3
- tile_count: int32 [8, 6, 4], P('blk', None, 'split'), may hold values from 21 to 80
- user_count: int32 [8192], P('blk'), may hold values from 1 to 16
- item_count: int32 [16384], P(('blk', 'split')), may hold values from 1 to 64
- user_factors: float32 [8192, 128], P('blk'), may hold values from -0.1502602 to 0.1502602
- item_factors: float32 [16384, 128], P(('blk', 'split')), may hold values from -0.1502602 to 0.1502602
Outputs:
- users_out: float32 [8192, 128], P('blk')
- items_out: float32 [16384, 128], P(('blk', 'split'))
The draws below stay inside these ranges and needn't reach their ends.
Inputs may be any that keep to these rules, and one draw needn't show every extreme that they name: Only the first tile_count slots of a list hold ratings; the rest are ignored.
All inputs are finite; a program needn't handle non-finite values.
Results may differ from the reference program's by a relative error of at most 0.00078.
Values sent between devices are 32-bit elements; how exact they have to be, the bound alone decides.
A program may use at most 128 MiB of HBM per device.

```python
import math
import jax
import jax.numpy as jnp
import numpy as np
from jax import lax

R = 128
TILE = 128
UB = 1024
PANEL = 2048
VISITS = 6
TD = 80
USERS = 8192
ITEMS = 16384
N_BLK = 8
N_SPLIT = 4


def plant(entries, stream_key, least, top_value):
    dims = entries.shape
    place = [jax.random.randint(jax.random.fold_in(stream_key, axis), (), 0, dims[axis]) for axis in range(len(dims))]
    entries = entries.at[tuple(place)].set(least)
    longest = dims.index(max(dims))
    place[longest] = (place[longest] + 1) % dims[longest]
    return entries.at[tuple(place)].set(top_value)


def level_of(stream_key, shape, cuts, least, top_value):
    level = 1.0
    for position, parts in cuts:
        heights = jax.random.uniform(jax.random.fold_in(jax.random.fold_in(stream_key, 6), position), (parts,), jnp.float32, least / len(cuts), top_value / len(cuts))
        level = level * jnp.repeat(jnp.exp(heights), shape[position] // parts).reshape((-1,) + (1,) * (len(shape) - 1 - position))
    return level


def rank_bounds(amount, skew):
    weights = [(1 << 20) // math.isqrt(rank ** skew) + 1 for rank in range(1, amount + 1)]
    deviation = 1 + sum(weights) // (1 << 30)
    return np.cumsum(np.array([max(1, weight // deviation) for weight in weights]))


def ranked_ids(stream_key, shape, amount, skew):
    grid = rank_bounds(amount, skew)
    lot = jax.random.randint(jax.random.fold_in(stream_key, 1), shape, 0, int(grid[amount - 1]))
    grade = jnp.searchsorted(jnp.asarray(grid, jnp.int32), lot, side="right")
    return jax.random.permutation(jax.random.fold_in(stream_key, 2), amount)[grade].astype(jnp.int32)


def noise(rng, extent, scale, limit, pieces=(), held_as=jnp.bfloat16):
    gain = level_of(rng, extent, pieces, -0.22, 0.18) if pieces else 1.0
    entries = jax.random.normal(rng, extent, jnp.float32) * scale * gain
    return jnp.minimum(jnp.maximum(entries, -limit), limit).astype(held_as)


def setup_inputs(seed: int = 0) -> dict:
    arg_keys = jax.random.split(jax.random.key(seed), 9)
    return {
        "ratings": noise(arg_keys[0], (N_BLK, VISITS, N_SPLIT, TD, TILE, TILE), 1.0, 6.0, ((0, 8), (2, 4))),
        "user_tile": plant(ranked_ids(arg_keys[1], (N_BLK, VISITS, N_SPLIT, TD), UB // TILE, 4), jax.random.fold_in(arg_keys[1], 3), 0, (UB // TILE) - 1).astype(jnp.int32),
        "item_tile": plant(jax.random.randint(arg_keys[2], (N_BLK, VISITS, N_SPLIT, TD), 0, PANEL // (N_SPLIT * TILE)), jax.random.fold_in(arg_keys[2], 1), 0, (PANEL // (N_SPLIT * TILE)) - 1).astype(jnp.int32),
        "tile_count": plant(jax.random.randint(arg_keys[3], (N_BLK, VISITS, N_SPLIT), TD // 4 + 1, TD + 1), jax.random.fold_in(arg_keys[3], 1), TD // 4 + 1, TD).astype(jnp.int32),
        "user_count": plant(jax.random.randint(arg_keys[4], (USERS,), 1, 17), jax.random.fold_in(arg_keys[4], 1), 1, 16).astype(jnp.int32),
        "item_count": plant(jax.random.randint(arg_keys[5], (ITEMS,), 1, 65), jax.random.fold_in(arg_keys[5], 1), 1, 64).astype(jnp.int32),
        "user_factors": jnp.clip(jax.random.uniform(arg_keys[6], (USERS, R), jnp.float32, -0.1502602, 0.1502602) * level_of(arg_keys[6], (USERS, R), ((0, 8),), -0.4, 0.0), -0.1502602, 0.1502602),
        "item_factors": jnp.clip(jax.random.uniform(arg_keys[7], (ITEMS, R), jnp.float32, -0.1502602, 0.1502602) * level_of(arg_keys[7], (ITEMS, R), ((0, 32),), -0.4, 0.0), -0.1502602, 0.1502602),
    }


step_gain = 12.0
decay_rate = 0.05

def reference(ratings, user_tile, item_tile, tile_count, user_count, item_count, user_factors, item_factors):
    part_len = PANEL // N_SPLIT
    user_tiles = UB // TILE
    item_tiles = part_len // TILE
    user_norm = TD * TILE * TILE * N_SPLIT / UB
    item_norm = TD * TILE * TILE * N_SPLIT / PANEL
    user_step = (step_gain / (user_norm * jnp.sqrt(user_count.astype(jnp.float32)))).reshape(N_BLK, UB)
    item_step = (step_gain / (item_norm * jnp.sqrt(item_count.astype(jnp.float32)))).reshape(N_BLK, N_SPLIT, part_len)
    user_rows = user_factors.reshape(N_BLK, UB, R)
    item_rows = item_factors.reshape(N_BLK, N_SPLIT, part_len, R)
    highest = lax.Precision.HIGHEST
    for visit_no in range(VISITS):
        panels = jnp.roll(item_rows, -visit_no, axis=0)
        panel_steps = jnp.roll(item_step, -visit_no, axis=0)

        def one_block(inputs):
            tile_vals, user_idx, item_idx, live_count, block_rows, block_step, panel_rows, panel_step = inputs
            user_half = block_rows.astype(jnp.bfloat16).reshape(user_tiles, TILE, R)

            def split_work(vals_s, uidx_s, iidx_s, count_s, part_rows):
                item_half = part_rows.astype(jnp.bfloat16).reshape(item_tiles, TILE, R)
                user_sel = user_half[uidx_s].astype(jnp.float32)
                item_sel = item_half[iidx_s].astype(jnp.float32)
                predicted = jnp.einsum('tur,tir->tui', user_sel, item_sel, precision=highest)
                live_mask = (jnp.arange(TD) < count_s).astype(jnp.float32)
                residual = (live_mask[:, None, None] * (vals_s.astype(jnp.float32) - predicted)).astype(jnp.bfloat16)
                res_wide = residual.astype(jnp.float32)
                grad_user_t = jnp.einsum('tui,tir->tur', res_wide, item_sel, precision=highest)
                grad_item_t = jnp.einsum('tui,tur->tir', res_wide, user_sel, precision=highest)
                grad_user = jax.ops.segment_sum(grad_user_t, uidx_s, user_tiles).reshape(UB, R)
                grad_item = jax.ops.segment_sum(grad_item_t, iidx_s, item_tiles).reshape(part_len, R)
                return (grad_user, grad_item)
            user_parts, grad_items = jax.vmap(split_work)(tile_vals, user_idx, item_idx, live_count, panel_rows)
            grad_user = lax.optimization_barrier(jnp.sum(user_parts, axis=0))
            new_block = block_rows + block_step[:, None] * (grad_user - decay_rate * block_rows)
            new_panel = panel_rows + panel_step[..., None] * (grad_items - decay_rate * panel_rows)
            return (new_block, new_panel)
        new_users, new_panels = lax.map(one_block, (ratings[:, visit_no], user_tile[:, visit_no], item_tile[:, visit_no], tile_count[:, visit_no], user_rows, user_step, panels, panel_steps))
        user_rows = new_users
        item_rows = jnp.roll(new_panels, visit_no, axis=0)
    return (user_rows.reshape(UB * N_BLK, R), item_rows.reshape(PANEL * N_BLK, R))
```

```python
import functools

import jax
import jax.numpy as jnp
from jax import lax
from jax.experimental import pallas as pl
from jax.experimental.pallas import tpu as pltpu
from jax.sharding import PartitionSpec as P

MESH = pl.DeviceIdType.MESH
step_gain = 12.0
decay_rate = 0.05
PAD = 8


def chain_cells(item_tiles, cell_total, user_idx, item_idx, live_count):
    slots = user_idx.shape[1]
    at = jnp.arange(slots)
    live = at[None, :] < live_count[:, None]
    cell = jnp.where(live, user_idx * item_tiles + item_idx, cell_total)
    number = (at + 1)[None, None, :]
    same = (cell[:, :, None] == cell[:, None, :]) & (at[:, None] > at[None, :])[None]
    before = jnp.max(jnp.where(same, number, 0), axis=2)
    held = cell[:, None, :] == jnp.arange(cell_total)[None, :, None]
    last = jnp.max(jnp.where(held, number, 0), axis=2)
    counts = jnp.sum(held.astype(jnp.float32), axis=2)
    return before.astype(jnp.int32), last.astype(jnp.int32), counts


def column(row, width):
    return jnp.broadcast_to(row, (width, row.shape[1])).T


def run_visits(
    sizes, before, last, counts, ratings, user_count, item_count, user_in, panel_in, user_out, panel_out,
    u, ustep, g, fold, peer, vp, v16, gi, tiles, sums,
    g_sent, fold_got, peer_got, u_sent, u_got, v_sent, v_got, tiles_got,
):
    visits, n_blk, n_split, ch, group, lag, user_gain, item_gain = sizes
    slots, tile = ratings.shape[1], ratings.shape[-1]
    users, width = user_in.shape
    part = panel_in.shape[0]
    item_tiles = part // tile
    chunks = users // ch
    rows_of = group * ch // tile
    cells_of = rows_of * item_tiles
    f32, bf16 = jnp.float32, jnp.bfloat16

    b, s = lax.axis_index("blk"), lax.axis_index("split")
    half = n_split // 2
    left_side = s < half
    inward = jnp.where(left_side, s + 1, s - 1)
    outward = jnp.where(left_side, s - 1, s + 1)
    middle = (s == half - 1) | (s == half)
    has_outer = (s > 0) & (s < n_split - 1)
    back = lax.rem(b + n_blk - 1, n_blk)
    front = lax.rem(b + 1, n_blk)
    home = lax.rem(b + visits - 1, n_blk)
    guest = lax.rem(b + n_blk * visits - (visits - 1), n_blk)

    barrier = pltpu.get_barrier_semaphore()
    for other in (back, front, home, guest):
        pl.semaphore_signal(barrier, inc=1, device_id={"blk": other}, device_id_type=MESH)
    pl.semaphore_signal(barrier, inc=1, device_id={"split": inward}, device_id_type=MESH)

    @pl.when(has_outer)
    def _():
        pl.semaphore_signal(barrier, inc=1, device_id={"split": outward}, device_id_type=MESH)

    def rows(k):
        return pl.ds(pl.multiple_of(k * ch, ch), ch)

    def tiles_copy(v):
        slot = lax.rem(v, 2)
        return pltpu.make_async_copy(ratings.at[v], tiles.at[slot], tiles_got.at[slot])

    def add_tiles(v, lo, hi):
        slot = lax.rem(v, 2)

        def add(t, carry):
            sums[t + 1] = tiles[slot, t].astype(f32) + sums[before[v, t]]
            return carry

        lax.fori_loop(lo, hi, add, 0)

    def fold_copy(k):
        return pltpu.make_async_remote_copy(
            src_ref=g.at[rows(k)], dst_ref=fold.at[rows(k)], send_sem=g_sent.at[k],
            recv_sem=fold_got.at[k], device_id={"split": inward}, device_id_type=MESH)

    def peer_copy(v, k):
        par = lax.rem(v, 2)
        return pltpu.make_async_remote_copy(
            src_ref=g.at[rows(k)], dst_ref=peer.at[par, rows(k)], send_sem=g_sent.at[k],
            recv_sem=peer_got.at[par, k], device_id={"split": inward}, device_id_type=MESH)

    def user_copy(k):
        return pltpu.make_async_remote_copy(
            src_ref=u.at[rows(k)], dst_ref=u.at[rows(k)], send_sem=u_sent.at[k],
            recv_sem=u_got.at[k], device_id={"split": outward}, device_id_type=MESH)

    def panel_copy(v, to):
        return pltpu.make_async_remote_copy(
            src_ref=vp.at[v], dst_ref=vp.at[v + 1], send_sem=v_sent.at[v],
            recv_sem=v_got.at[v], device_id={"blk": to}, device_id_type=MESH)

    tiles_copy(0).start()
    if visits > 1:
        tiles_copy(1).start()
    sums[0] = jnp.zeros(sums.shape[1:], f32)
    u[...] = user_in[...]
    vp[0, :part] = panel_in[...]
    item_step = item_gain / jnp.sqrt(item_count[...].astype(f32))
    vp[0, part:] = jnp.concatenate(
        [item_step, jnp.zeros((vp.shape[1] - part - item_step.shape[0], width), f32)], axis=0)
    user_step = user_gain / jnp.sqrt(user_count[...].astype(f32))
    for a in range(users // tile):
        ustep[a * tile:(a + 1) * tile] = column(user_step[a:a + 1], width)
    tiles_copy(0).wait()
    add_tiles(0, 0, slots)
    pl.semaphore_wait(barrier, jnp.where(has_outer, 6, 5))

    def grads(v, q):
        of = pl.ds(pl.multiple_of(q * group * ch, group * ch), group * ch)
        user_half = u[of].astype(bf16)
        items = v16[...]
        predicted = lax.dot_general(
            user_half, items, (((1,), (1,)), ((), ())), preferred_element_type=f32)
        high, low = [], []
        for a in range(rows_of):
            hs, ls = [], []
            for j in range(item_tiles):
                c = q * cells_of + a * item_tiles + j
                err = sums[last[v, c]] - counts[v, c] * predicted[
                    a * tile:(a + 1) * tile, j * tile:(j + 1) * tile]
                h = err.astype(bf16)
                hs.append(h)
                ls.append((err - h.astype(f32)).astype(bf16))
            high.append(jnp.concatenate(hs, axis=1))
            low.append(jnp.concatenate(ls, axis=1))
        high, low = jnp.concatenate(high, axis=0), jnp.concatenate(low, axis=0)
        gu = jnp.dot(high, items, preferred_element_type=f32)
        gu += jnp.dot(low, items, preferred_element_type=f32)
        over = (((0,), (0,)), ((), ()))
        gi[...] += lax.dot_general(user_half, high, over, preferred_element_type=f32) + lax.dot_general(
            user_half, low, over, preferred_element_type=f32)

        @pl.when(v > 0)
        def _():
            for k in range(group):
                fold_copy(q * group + k).wait_send()

        g[of] = gu

        @pl.when(jnp.logical_not(has_outer))
        def _():
            for k in range(group):
                send_in(v, q * group + k)

    def send_in(v, k):
        @pl.when(middle)
        def _():
            peer_copy(v, k).start()

        @pl.when(jnp.logical_not(middle))
        def _():
            fold_copy(k).start()

    def pass_in(v, k):
        fold_copy(k).wait_recv()
        g[rows(k)] += fold[rows(k)]
        send_in(v, k)

    def settle(v, k):
        @pl.when(middle)
        def _():
            peer_copy(v, k).wait_recv()

            @pl.when(has_outer & (v > 0))
            def _():
                user_copy(k).wait_send()

            old = u[rows(k)]
            grad = g[rows(k)] + peer[lax.rem(v, 2), rows(k)]
            u[rows(k)] = old + ustep[rows(k)] * (grad - decay_rate * old)

        @pl.when(jnp.logical_not(middle))
        def _():
            @pl.when(has_outer & (v > 0))
            def _():
                user_copy(k).wait_send()

            user_copy(k).wait_recv()

        @pl.when(has_outer)
        def _():
            user_copy(k).start()

    def loop(lo, hi, step):
        def body(k, carry):
            step(k)
            return carry

        lax.fori_loop(lo, hi, body, 0)

    groups = chunks // group
    ahead = group * (groups - 2)
    tail = chunks - group - ahead

    def step(i):
        @pl.when(i < visits * chunks)
        def _():
            pass_in(i // chunks, i % chunks)

        @pl.when(i >= lag)
        def _():
            settle((i - lag) // chunks, (i - lag) % chunks)

    def between(v, q):
        if q < groups - 1:
            @pl.when(has_outer)
            def _():
                first = v * chunks - tail
                share = tail // (groups - 2)
                loop(first + (q - 1) * share, first + q * share, step)

        @pl.when(jnp.logical_not(has_outer))
        def _():
            loop(q * group, (q + 1) * group, lambda k: settle(v - 1, k))

    def visit(v, carry):
        @pl.when(v > 0)
        def _():
            panel_copy(v - 1, back).wait_recv()

        v16[...] = vp[v, :part].astype(bf16)
        gi[...] = jnp.zeros_like(gi)
        grads(v, 0)
        for q in range(1, groups):
            @pl.when(v > 0)
            def _():
                between(v, q)

            if q == groups - 1:
                @pl.when(has_outer)
                def _():
                    loop(0, group, lambda k: step(v * chunks + k))

            grads(v, q)

        for j in range(item_tiles):
            at = slice(j * tile, (j + 1) * tile)
            old = vp[v, at]
            vp[v, at] = old + column(vp[v, part + j:part + j + 1], width) * (
                gi[:, at].T - decay_rate * old)

        @pl.when(v < visits - 1)
        def _():
            panel_copy(v, back).start()

        @pl.when(v == visits - 1)
        def _():
            panel_copy(v, home).start()

        @pl.when(v + 1 < visits)
        def _():
            tiles_copy(v + 1).wait()

        @pl.when(v + 2 < visits)
        def _():
            tiles_copy(v + 2).start()

        @pl.when(has_outer)
        def _():
            def early(k):
                step(v * chunks + group + k)

                @pl.when(v + 1 < visits)
                def _():
                    add_tiles(v + 1, k * slots // ahead, (k + 1) * slots // ahead)

            loop(0, ahead, early)

        @pl.when(jnp.logical_not(has_outer))
        def _():
            @pl.when(v + 1 < visits)
            def _():
                add_tiles(v + 1, 0, slots)

            loop(0, group, lambda k: settle(v, k))

        return carry

    lax.fori_loop(0, visits, visit, 0)

    @pl.when(has_outer)
    def _():
        loop(visits * chunks - tail, visits * chunks + lag, step)

    @pl.when(jnp.logical_not(has_outer))
    def _():
        loop(group, chunks, lambda k: settle(visits - 1, k))

    user_out[...] = u[...]
    panel_copy(visits - 1, home).wait_recv()
    panel_out[...] = vp[visits, :part]
    loop(0, visits, lambda v: panel_copy(v, back).wait_send())
    loop(0, chunks, lambda k: fold_copy(k).wait_send())

    @pl.when(has_outer)
    def _():
        loop(0, chunks, lambda k: user_copy(k).wait_send())


def per_device(
    n_blk, n_split,
    ratings, user_tile, item_tile, tile_count, user_count, item_count, user_factors, item_factors
):
    visits, slots, tile = ratings.shape[1], ratings.shape[3], ratings.shape[-1]
    users, width = user_factors.shape
    part = item_factors.shape[0]
    user_tiles, item_tiles = users // tile, part // tile
    cell_total = user_tiles * item_tiles
    f32 = jnp.float32
    vmem = pl.BlockSpec(memory_space=pltpu.VMEM)
    smem = pl.BlockSpec(memory_space=pltpu.SMEM)

    before, last, counts = chain_cells(
        item_tiles, cell_total, user_tile.reshape(visits, slots), item_tile.reshape(visits, slots),
        tile_count.reshape(visits))
    ch = tile // 2
    chunks = users // ch
    user_gain = step_gain * users / (slots * tile * tile * n_split)
    item_gain = step_gain * part / (slots * tile * tile)
    group = 4
    sizes = (visits, n_blk, n_split, ch, group, group - 1, user_gain, item_gain)
    dma = pltpu.SemaphoreType.DMA
    return pl.pallas_call(
        functools.partial(run_visits, sizes),
        out_shape=[
            jax.ShapeDtypeStruct((users, width), f32),
            jax.ShapeDtypeStruct((part, width), f32),
        ],
        in_specs=[smem, smem, smem, pl.BlockSpec(memory_space=pl.ANY), vmem, vmem, vmem, vmem],
        out_specs=[vmem, vmem],
        scratch_shapes=[
            pltpu.VMEM((users, width), f32),
            pltpu.VMEM((users, width), f32),
            pltpu.VMEM((users, width), f32),
            pltpu.VMEM((users, width), f32),
            pltpu.VMEM((2, users, width), f32),
            pltpu.VMEM((visits + 1, part + pl.cdiv(item_tiles, PAD) * PAD, width), f32),
            pltpu.VMEM((part, width), jnp.bfloat16),
            pltpu.VMEM((width, part), f32),
            pltpu.VMEM((2, slots, tile, tile), ratings.dtype),
            pltpu.VMEM((slots + 1, tile, tile), f32),
            dma((chunks,)), dma((chunks,)), dma((2, chunks)), dma((chunks,)), dma((chunks,)),
            dma((visits,)), dma((visits,)), dma((2,)),
        ],
        compiler_params=pltpu.CompilerParams(collective_id=0, has_side_effects=True),
        name="run_visits",
    )(
        before, last, counts, ratings.reshape(visits, slots, tile, tile), user_count.reshape(users // tile, tile),
        item_count.reshape(item_tiles, tile), user_factors, item_factors,
    )


def solution(mesh):
    return jax.shard_map(
        functools.partial(per_device, mesh.shape["blk"], mesh.shape["split"]),
        mesh=mesh,
        in_specs=(
            P("blk", None, "split", None, None, None),
            P("blk", None, "split", None),
            P("blk", None, "split", None),
            P("blk", None, "split"),
            P("blk"),
            P(("blk", "split")),
            P("blk", None),
            P(("blk", "split"), None),
        ),
        out_specs=(P("blk", None), P(("blk", "split"), None)),
        check_vma=False,
    )
```

```python
import functools

import jax
import jax.numpy as jnp
from jax import lax
from jax.experimental import pallas as pl
from jax.experimental.pallas import tpu as pltpu
from jax.sharding import PartitionSpec as P

MESH = pl.DeviceIdType.MESH
step_gain = 12.0
decay_rate = 0.05
PAD = 8


def chain_cells(item_tiles, cell_total, user_idx, item_idx, live_count):
    slots = user_idx.shape[1]
    at = jnp.arange(slots)
    live = at[None, :] < live_count[:, None]
    cell = jnp.where(live, user_idx * item_tiles + item_idx, cell_total)
    number = (at + 1)[None, None, :]
    same = (cell[:, :, None] == cell[:, None, :]) & (at[:, None] > at[None, :])[None]
    before = jnp.max(jnp.where(same, number, 0), axis=2)
    held = cell[:, None, :] == jnp.arange(cell_total)[None, :, None]
    last = jnp.max(jnp.where(held, number, 0), axis=2)
    counts = jnp.sum(held.astype(jnp.float32), axis=2)
    return before.astype(jnp.int32), last.astype(jnp.int32), counts


def column(row, width):
    return jnp.broadcast_to(row, (width, row.shape[1])).T


def run_visits(
    sizes, before, last, counts, ratings, user_count, item_count, user_in, panel_in, user_out, panel_out,
    u, ustep, g, fold, peer, vp, v16, gi, tiles, sums,
    g_sent, fold_got, peer_got, u_sent, u_got, v_sent, v_got, tiles_got,
):
    visits, n_blk, n_split, ch, group, lag, user_gain, item_gain = sizes
    slots, tile = ratings.shape[1], ratings.shape[-1]
    users, width = user_in.shape
    part = panel_in.shape[0]
    item_tiles = part // tile
    chunks = users // ch
    rows_of = group * ch // tile
    cells_of = rows_of * item_tiles
    f32, bf16 = jnp.float32, jnp.bfloat16

    b, s = lax.axis_index("blk"), lax.axis_index("split")
    half = n_split // 2
    left_side = s < half
    inward = jnp.where(left_side, s + 1, s - 1)
    outward = jnp.where(left_side, s - 1, s + 1)
    middle = (s == half - 1) | (s == half)
    has_outer = (s > 0) & (s < n_split - 1)
    back = lax.rem(b + n_blk - 1, n_blk)
    front = lax.rem(b + 1, n_blk)
    home = lax.rem(b + visits - 1, n_blk)
    guest = lax.rem(b + n_blk * visits - (visits - 1), n_blk)

    barrier = pltpu.get_barrier_semaphore()
    for other in (back, front, home, guest):
        pl.semaphore_signal(barrier, inc=1, device_id={"blk": other}, device_id_type=MESH)
    pl.semaphore_signal(barrier, inc=1, device_id={"split": inward}, device_id_type=MESH)

    @pl.when(has_outer)
    def _():
        pl.semaphore_signal(barrier, inc=1, device_id={"split": outward}, device_id_type=MESH)

    def rows(k):
        return pl.ds(pl.multiple_of(k * ch, ch), ch)

    def tiles_copy(v):
        slot = lax.rem(v, 2)
        return pltpu.make_async_copy(ratings.at[v], tiles.at[slot], tiles_got.at[slot])

    def add_tiles(v, lo, hi):
        slot = lax.rem(v, 2)

        def add(t, carry):
            sums[t + 1] = tiles[slot, t].astype(f32) + sums[before[v, t]]
            return carry

        lax.fori_loop(lo, hi, add, 0)

    def fold_copy(k):
        return pltpu.make_async_remote_copy(
            src_ref=g.at[rows(k)], dst_ref=fold.at[rows(k)], send_sem=g_sent.at[k],
            recv_sem=fold_got.at[k], device_id={"split": inward}, device_id_type=MESH)

    def peer_copy(v, k):
        par = lax.rem(v, 2)
        return pltpu.make_async_remote_copy(
            src_ref=g.at[rows(k)], dst_ref=peer.at[par, rows(k)], send_sem=g_sent.at[k],
            recv_sem=peer_got.at[par, k], device_id={"split": inward}, device_id_type=MESH)

    def user_copy(k):
        return pltpu.make_async_remote_copy(
            src_ref=u.at[rows(k)], dst_ref=u.at[rows(k)], send_sem=u_sent.at[k],
            recv_sem=u_got.at[k], device_id={"split": outward}, device_id_type=MESH)

    def panel_copy(v, j, to):
        end = vp.shape[1] if j == item_tiles - 1 else (j + 1) * tile
        at = pl.ds(j * tile, end - j * tile)
        return pltpu.make_async_remote_copy(
            src_ref=vp.at[v, at], dst_ref=vp.at[v + 1, at], send_sem=v_sent.at[v, j],
            recv_sem=v_got.at[v, j], device_id={"blk": to}, device_id_type=MESH)

    tiles_copy(0).start()
    if visits > 1:
        tiles_copy(1).start()
    sums[0] = jnp.zeros(sums.shape[1:], f32)
    u[...] = user_in[...]
    vp[0, :part] = panel_in[...]
    item_step = item_gain / jnp.sqrt(item_count[...].astype(f32))
    vp[0, part:] = jnp.concatenate(
        [item_step, jnp.zeros((vp.shape[1] - part - item_step.shape[0], width), f32)], axis=0)
    user_step = user_gain / jnp.sqrt(user_count[...].astype(f32))
    for a in range(users // tile):
        ustep[a * tile:(a + 1) * tile] = column(user_step[a:a + 1], width)
    tiles_copy(0).wait()
    add_tiles(0, 0, slots)
    pl.semaphore_wait(barrier, jnp.where(has_outer, 6, 5))

    def grads(v, q):
        of = pl.ds(pl.multiple_of(q * group * ch, group * ch), group * ch)
        user_half = u[of].astype(bf16)
        items = v16[...]
        predicted = lax.dot_general(
            user_half, items, (((1,), (1,)), ((), ())), preferred_element_type=f32)
        high, low = [], []
        for a in range(rows_of):
            hs, ls = [], []
            for j in range(item_tiles):
                c = q * cells_of + a * item_tiles + j
                err = sums[last[v, c]] - counts[v, c] * predicted[
                    a * tile:(a + 1) * tile, j * tile:(j + 1) * tile]
                h = err.astype(bf16)
                hs.append(h)
                ls.append((err - h.astype(f32)).astype(bf16))
            high.append(jnp.concatenate(hs, axis=1))
            low.append(jnp.concatenate(ls, axis=1))
        high, low = jnp.concatenate(high, axis=0), jnp.concatenate(low, axis=0)
        gu = jnp.dot(high, items, preferred_element_type=f32)
        gu += jnp.dot(low, items, preferred_element_type=f32)
        @pl.when(v > 0)
        def _():
            for k in range(group):
                fold_copy(q * group + k).wait_send()

        g[of] = gu

        @pl.when(jnp.logical_not(has_outer))
        def _():
            for k in range(group):
                send_in(v, q * group + k)

        over = (((0,), (0,)), ((), ()))
        gi[...] += lax.dot_general(user_half, high, over, preferred_element_type=f32) + lax.dot_general(
            user_half, low, over, preferred_element_type=f32)

    def send_in(v, k):
        @pl.when(middle)
        def _():
            peer_copy(v, k).start()

        @pl.when(jnp.logical_not(middle))
        def _():
            fold_copy(k).start()

    def pass_in(v, k):
        fold_copy(k).wait_recv()
        g[rows(k)] += fold[rows(k)]
        send_in(v, k)

    def settle(v, k):
        @pl.when(middle)
        def _():
            peer_copy(v, k).wait_recv()

            @pl.when(has_outer & (v > 0))
            def _():
                user_copy(k).wait_send()

            old = u[rows(k)]
            grad = g[rows(k)] + peer[lax.rem(v, 2), rows(k)]
            u[rows(k)] = old + ustep[rows(k)] * (grad - decay_rate * old)

        @pl.when(jnp.logical_not(middle))
        def _():
            @pl.when(has_outer & (v > 0))
            def _():
                user_copy(k).wait_send()

            user_copy(k).wait_recv()

        @pl.when(has_outer)
        def _():
            user_copy(k).start()

    def loop(lo, hi, step):
        def body(k, carry):
            step(k)
            return carry

        lax.fori_loop(lo, hi, body, 0)

    groups = chunks // group
    behind = groups - 1 - lag
    rest = chunks - groups

    def step(i):
        @pl.when((i >= 0) & (i < visits * chunks))
        def _():
            pass_in(i // chunks, i % chunks)

        @pl.when(i >= lag)
        def _():
            settle((i - lag) // chunks, (i - lag) % chunks)

    def visit(v, carry):
        @pl.when(v > 0)
        def _():
            for j in range(item_tiles):
                at = slice(j * tile, (j + 1) * tile)
                panel_copy(v - 1, j, back).wait_recv()
                v16[at] = vp[v, at].astype(bf16)

        @pl.when(v == 0)
        def _():
            v16[...] = vp[0, :part].astype(bf16)

        gi[...] = jnp.zeros_like(gi)

        def turn(q):
            @pl.when(jnp.logical_not(has_outer) & (v > 0))
            def _():
                for k in range(group):
                    settle(v - 1, q * group + k)

            grads(v, q)

            @pl.when(has_outer)
            def _():
                step(v * chunks - behind + q)

        loop(0, groups, turn)
        for j in range(item_tiles):
            at = slice(j * tile, (j + 1) * tile)
            old = vp[v, at]
            vp[v, at] = old + column(vp[v, part + j:part + j + 1], width) * (
                gi[:, at].T - decay_rate * old)

            @pl.when(v < visits - 1)
            def _():
                panel_copy(v, j, back).start()

            @pl.when(v == visits - 1)
            def _():
                panel_copy(v, j, home).start()

        @pl.when(v + 1 < visits)
        def _():
            tiles_copy(v + 1).wait()

        @pl.when(v + 2 < visits)
        def _():
            tiles_copy(v + 2).start()

        @pl.when(has_outer)
        def _():
            def early(k):
                step(v * chunks - behind + groups + k)

                @pl.when(v + 1 < visits)
                def _():
                    add_tiles(v + 1, k * slots // rest, (k + 1) * slots // rest)

            loop(0, rest, early)

        @pl.when(jnp.logical_not(has_outer))
        def _():
            @pl.when(v + 1 < visits)
            def _():
                add_tiles(v + 1, 0, slots)

        return carry

    lax.fori_loop(0, visits, visit, 0)

    @pl.when(has_outer)
    def _():
        loop(visits * chunks - behind, visits * chunks + lag, step)

    @pl.when(jnp.logical_not(has_outer))
    def _():
        loop(0, chunks, lambda k: settle(visits - 1, k))

    user_out[...] = u[...]
    for j in range(item_tiles):
        panel_copy(visits - 1, j, home).wait_recv()
        loop(0, visits, lambda v: panel_copy(v, j, back).wait_send())
    panel_out[...] = vp[visits, :part]
    loop(0, chunks, lambda k: fold_copy(k).wait_send())

    @pl.when(has_outer)
    def _():
        loop(0, chunks, lambda k: user_copy(k).wait_send())


def per_device(
    n_blk, n_split,
    ratings, user_tile, item_tile, tile_count, user_count, item_count, user_factors, item_factors
):
    visits, slots, tile = ratings.shape[1], ratings.shape[3], ratings.shape[-1]
    users, width = user_factors.shape
    part = item_factors.shape[0]
    user_tiles, item_tiles = users // tile, part // tile
    cell_total = user_tiles * item_tiles
    f32 = jnp.float32
    vmem = pl.BlockSpec(memory_space=pltpu.VMEM)
    smem = pl.BlockSpec(memory_space=pltpu.SMEM)

    before, last, counts = chain_cells(
        item_tiles, cell_total, user_tile.reshape(visits, slots), item_tile.reshape(visits, slots),
        tile_count.reshape(visits))
    ch = tile // 2
    chunks = users // ch
    user_gain = step_gain * users / (slots * tile * tile * n_split)
    item_gain = step_gain * part / (slots * tile * tile)
    group, lag = 2, 5
    sizes = (visits, n_blk, n_split, ch, group, lag, user_gain, item_gain)
    dma = pltpu.SemaphoreType.DMA
    return pl.pallas_call(
        functools.partial(run_visits, sizes),
        out_shape=[
            jax.ShapeDtypeStruct((users, width), f32),
            jax.ShapeDtypeStruct((part, width), f32),
        ],
        in_specs=[smem, smem, smem, pl.BlockSpec(memory_space=pl.ANY), vmem, vmem, vmem, vmem],
        out_specs=[vmem, vmem],
        scratch_shapes=[
            pltpu.VMEM((users, width), f32),
            pltpu.VMEM((users, width), f32),
            pltpu.VMEM((users, width), f32),
            pltpu.VMEM((users, width), f32),
            pltpu.VMEM((2, users, width), f32),
            pltpu.VMEM((visits + 1, part + pl.cdiv(item_tiles, PAD) * PAD, width), f32),
            pltpu.VMEM((part, width), jnp.bfloat16),
            pltpu.VMEM((width, part), f32),
            pltpu.VMEM((2, slots, tile, tile), ratings.dtype),
            pltpu.VMEM((slots + 1, tile, tile), f32),
            dma((chunks,)), dma((chunks,)), dma((2, chunks)), dma((chunks,)), dma((chunks,)),
            dma((visits, item_tiles)), dma((visits, item_tiles)), dma((2,)),
        ],
        compiler_params=pltpu.CompilerParams(collective_id=0, has_side_effects=True),
        name="run_visits",
    )(
        before, last, counts, ratings.reshape(visits, slots, tile, tile), user_count.reshape(users // tile, tile),
        item_count.reshape(item_tiles, tile), user_factors, item_factors,
    )


def solution(mesh):
    return jax.shard_map(
        functools.partial(per_device, mesh.shape["blk"], mesh.shape["split"]),
        mesh=mesh,
        in_specs=(
            P("blk", None, "split", None, None, None),
            P("blk", None, "split", None),
            P("blk", None, "split", None),
            P("blk", None, "split"),
            P("blk"),
            P(("blk", "split")),
            P("blk", None),
            P(("blk", "split"), None),
        ),
        out_specs=(P("blk", None), P(("blk", "split"), None)),
        check_vma=False,
    )
```

```python
import functools

import jax
import jax.numpy as jnp
from jax import lax
from jax.experimental import pallas as pl
from jax.experimental.pallas import tpu as pltpu
from jax.sharding import PartitionSpec as P

MESH = pl.DeviceIdType.MESH
step_gain = 12.0
decay_rate = 0.05
PAD = 8
LANES = 128
PIECES = 4


def column(row, width):
    return jnp.broadcast_to(row, (width, row.shape[1])).T


def run_visits(
    sizes, tile_count, user_tile, item_tile, ratings, user_count, item_count, user_in, panel_in, user_out, panel_out,
    u, ustep, g, fold, peer, vp, v16, v16t, gi, tiles, sums, key, chain_v, live_v, chain, live, turn_v,
    g_sent, fold_got, peer_got, u_sent, u_got, v_sent, v_got, tiles_got, chain_got, in_got, out_sent,
):
    visits, n_blk, n_split, ch, group, lag, pace, user_gain, item_gain = sizes
    slots, tile = ratings.shape[1], ratings.shape[-1]
    users, width = user_in.shape
    part = panel_in.shape[0]
    item_tiles = part // tile
    chunks = users // ch
    rows_of = group * ch // tile
    cells_of = rows_of * item_tiles
    f32, bf16 = jnp.float32, jnp.bfloat16

    b, s = lax.axis_index("blk"), lax.axis_index("split")
    half = n_split // 2
    left_side = s < half
    inward = jnp.where(left_side, s + 1, s - 1)
    outward = jnp.where(left_side, s - 1, s + 1)
    middle = (s == half - 1) | (s == half)
    has_outer = (s > 0) & (s < n_split - 1)
    back = lax.rem(b + n_blk - 1, n_blk)
    front = lax.rem(b + 1, n_blk)
    home = lax.rem(b + visits - 1, n_blk)
    guest = lax.rem(b + n_blk * visits - (visits - 1), n_blk)

    barrier = pltpu.get_barrier_semaphore()
    for other in (back, front, home, guest):
        pl.semaphore_signal(barrier, inc=1, device_id={"blk": other}, device_id_type=MESH)
    pl.semaphore_signal(barrier, inc=1, device_id={"split": inward}, device_id_type=MESH)

    @pl.when(has_outer)
    def _():
        pl.semaphore_signal(barrier, inc=1, device_id={"split": outward}, device_id_type=MESH)

    def rows(k):
        return pl.ds(pl.multiple_of(k * ch, ch), ch)

    def tiles_copy(v, i):
        slot, of = lax.rem(v, 2), pl.ds(i * slots // PIECES, (i + 1) * slots // PIECES - i * slots // PIECES)
        return pltpu.make_async_copy(ratings.at[v, of], tiles.at[slot, of], tiles_got.at[slot, i])

    def start_tiles(v):
        for i in range(PIECES):
            tiles_copy(v, i).start()

    def out_copy(k):
        return pltpu.make_async_copy(u.at[rows(k)], user_out.at[rows(k)], out_sent.at[k])

    def panel_out_copy(j):
        of = pl.ds(j * tile, tile)
        return pltpu.make_async_copy(turn_v.at[of], panel_out.at[of], out_sent.at[chunks + j])

    def add_tiles(v, lo, hi):
        slot = lax.rem(v, 2)

        def add(t, carry):
            sums[t + 1] = tiles[slot, t].astype(f32) + sums[chain[v, t]]
            return carry

        lax.fori_loop(lo, hi, add, 0)

    def fold_copy(k):
        return pltpu.make_async_remote_copy(
            src_ref=g.at[rows(k)], dst_ref=fold.at[rows(k)], send_sem=g_sent.at[k],
            recv_sem=fold_got.at[k], device_id={"split": inward}, device_id_type=MESH)

    def peer_copy(v, k):
        par = lax.rem(v, 2)
        return pltpu.make_async_remote_copy(
            src_ref=g.at[rows(k)], dst_ref=peer.at[par, rows(k)], send_sem=g_sent.at[k],
            recv_sem=peer_got.at[par, k], device_id={"split": inward}, device_id_type=MESH)

    def user_copy(k):
        return pltpu.make_async_remote_copy(
            src_ref=u.at[rows(k)], dst_ref=u.at[rows(k)], send_sem=u_sent.at[k],
            recv_sem=u_got.at[k], device_id={"split": outward}, device_id_type=MESH)

    def panel_copy(v, j, to):
        return pltpu.make_async_remote_copy(
            src_ref=vp.at[v, j], dst_ref=vp.at[v + 1, j], send_sem=v_sent.at[v, j],
            recv_sem=v_got.at[v, j], device_id={"blk": to}, device_id_type=MESH)

    start_tiles(0)
    in_copies = [
        pltpu.make_async_copy(user_in, u, in_got.at[0]), pltpu.make_async_copy(panel_in, turn_v, in_got.at[1])]
    for copy in in_copies:
        copy.start()
    if visits > 1:
        start_tiles(1)
    cell_total = users // tile * item_tiles
    lane = lax.broadcasted_iota(jnp.int32, key.shape, 1)
    key[...] = lane - slots
    at = lax.broadcasted_iota(jnp.int32, (1, slots), 1)
    for v in range(visits):
        cell = user_tile[v] * item_tiles + item_tile[v]
        key[v:v + 1, :slots] = jnp.where(at < tile_count[v], cell, cell_total)
    turned = key[...].T
    chain_v[...] = jnp.zeros_like(chain_v)
    live_v[...] = jnp.zeros_like(live_v)
    number = lax.broadcasted_iota(jnp.int32, (slots, key.shape[1]), 0)
    ahead = lax.broadcasted_iota(jnp.int32, number.shape, 1)
    ahead = jnp.minimum(ahead, slots)
    for v in range(visits):
        same = turned[:slots, v:v + 1] == key[v:v + 1]
        chain_v[v:v + 1] = jnp.max(
            jnp.where(same & (number < ahead), number + 1, 0), axis=0, keepdims=True)
        live_v[v:v + 1] = jnp.sum(jnp.where(same, 1.0, 0.0), axis=0, keepdims=True)
    chain_copies = [
        pltpu.make_async_copy(chain_v, chain, chain_got.at[0]), pltpu.make_async_copy(live_v, live, chain_got.at[1])]
    for copy in chain_copies:
        copy.start()
    sums[0] = jnp.zeros(sums.shape[1:], f32)
    item_step = item_gain / jnp.sqrt(item_count[...].astype(f32))
    user_step = user_gain / jnp.sqrt(user_count[...].astype(f32))
    for a in range(users // tile):
        ustep[a * tile:(a + 1) * tile] = column(user_step[a:a + 1], width)
    in_copies[1].wait()
    for j in range(item_tiles):
        vp[0, j, :width] = turn_v[j * tile:(j + 1) * tile].T
        vp[0, j, width:] = jnp.broadcast_to(item_step[j:j + 1], (PAD, tile))
    for copy in chain_copies:
        copy.wait()
    for i in range(PIECES):
        tiles_copy(0, i).wait()
        add_tiles(0, i * slots // PIECES, (i + 1) * slots // PIECES)
    in_copies[0].wait()
    pl.semaphore_wait(barrier, jnp.where(has_outer, 6, 5))

    def grads(v, q):
        of = pl.ds(pl.multiple_of(q * group * ch, group * ch), group * ch)
        user_half = u[of].astype(bf16)
        predicted = jnp.dot(user_half, v16t[...], preferred_element_type=f32)
        high, low = [], []
        for a in range(rows_of):
            hs, ls = [], []
            for j in range(item_tiles):
                c = q * cells_of + a * item_tiles + j
                err = sums[chain[v, slots + c]] - live[v, slots + c] * predicted[
                    a * tile:(a + 1) * tile, j * tile:(j + 1) * tile]
                h = err.astype(bf16)
                hs.append(h)
                ls.append((err - h.astype(f32)).astype(bf16))
            high.append(jnp.concatenate(hs, axis=1))
            low.append(jnp.concatenate(ls, axis=1))
        both = jnp.concatenate(high + low, axis=0)
        gu = jnp.dot(both, v16[...], preferred_element_type=f32)
        gu = gu[:group * ch] + gu[group * ch:]
        @pl.when(v > 0)
        def _():
            for k in range(group):
                fold_copy(q * group + k).wait_send()

        g[of] = gu

        @pl.when(jnp.logical_not(has_outer))
        def _():
            for k in range(group):
                send_in(v, q * group + k)

        over = (((0,), (0,)), ((), ()))
        twice = jnp.concatenate([user_half, user_half], axis=0)
        gi[...] += lax.dot_general(twice, both, over, preferred_element_type=f32)

    def send_in(v, k):
        @pl.when(middle)
        def _():
            peer_copy(v, k).start()

        @pl.when(jnp.logical_not(middle))
        def _():
            fold_copy(k).start()

    def pass_in(v, k):
        fold_copy(k).wait_recv()
        g[rows(k)] += fold[rows(k)]
        send_in(v, k)

    def settle(v, k):
        @pl.when(middle)
        def _():
            peer_copy(v, k).wait_recv()

            @pl.when(has_outer & (v > 0))
            def _():
                user_copy(k).wait_send()

            old = u[rows(k)]
            grad = g[rows(k)] + peer[lax.rem(v, 2), rows(k)]
            u[rows(k)] = old + ustep[rows(k)] * (grad - decay_rate * old)

        @pl.when(jnp.logical_not(middle))
        def _():
            @pl.when(has_outer & (v > 0))
            def _():
                user_copy(k).wait_send()

            user_copy(k).wait_recv()

        @pl.when(has_outer)
        def _():
            user_copy(k).start()

        @pl.when(v == visits - 1)
        def _():
            out_copy(k).start()

    def loop(lo, hi, step):
        def body(k, carry):
            step(k)
            return carry

        lax.fori_loop(lo, hi, body, 0)

    groups = chunks // group
    behind = pace * (groups - 1) - lag
    rest = chunks - pace * groups

    def step(i):
        @pl.when((i >= 0) & (i < visits * chunks))
        def _():
            pass_in(i // chunks, i % chunks)

        @pl.when(i >= lag)
        def _():
            settle((i - lag) // chunks, (i - lag) % chunks)

    def visit(v, carry):
        for j in range(item_tiles):
            @pl.when(v > 0)
            def _():
                panel_copy(v - 1, j, back).wait_recv()

            at = slice(j * tile, (j + 1) * tile)
            items = vp[v, j, :width]
            v16t[:, at] = items.astype(bf16)
            v16[at] = items.T.astype(bf16)

        gi[...] = jnp.zeros_like(gi)

        def turn(q):
            @pl.when(jnp.logical_not(has_outer) & (v > 0))
            def _():
                for k in range(group):
                    settle(v - 1, q * group + k)

            grads(v, q)

            @pl.when(has_outer)
            def _():
                for i in range(pace):
                    step(v * chunks - behind + q * pace + i)

        loop(0, groups, turn)
        for j in range(item_tiles):
            at = slice(j * tile, (j + 1) * tile)
            old = vp[v, j, :width]
            vp[v, j, :width] = old + vp[v, j, width:width + 1] * (gi[:, at] - decay_rate * old)

            @pl.when(v < visits - 1)
            def _():
                panel_copy(v, j, back).start()

            @pl.when(v == visits - 1)
            def _():
                panel_copy(v, j, home).start()

        @pl.when(v + 1 < visits)
        def _():
            for i in range(PIECES):
                tiles_copy(v + 1, i).wait()

        @pl.when(v + 2 < visits)
        def _():
            start_tiles(v + 2)

        @pl.when(has_outer)
        def _():
            def early(k):
                step(v * chunks - behind + groups * pace + k)

                @pl.when(v + 1 < visits)
                def _():
                    add_tiles(v + 1, k * slots // rest, (k + 1) * slots // rest)

            loop(0, rest, early)

        @pl.when(jnp.logical_not(has_outer))
        def _():
            @pl.when(v + 1 < visits)
            def _():
                add_tiles(v + 1, 0, slots)

        return carry

    lax.fori_loop(0, visits, visit, 0)

    @pl.when(has_outer)
    def _():
        loop(visits * chunks - behind, visits * chunks, step)

    @pl.when(jnp.logical_not(has_outer))
    def _():
        loop(0, chunks - group, lambda k: settle(visits - 1, k))

    for j in range(item_tiles):
        panel_copy(visits - 1, j, home).wait_recv()
        turn_v[j * tile:(j + 1) * tile] = vp[visits, j, :width].T
        panel_out_copy(j).start()

    @pl.when(has_outer)
    def _():
        loop(visits * chunks, visits * chunks + lag, step)

    @pl.when(jnp.logical_not(has_outer))
    def _():
        loop(chunks - group, chunks, lambda k: settle(visits - 1, k))

    for j in range(item_tiles):
        loop(0, visits, lambda v: panel_copy(v, j, back).wait_send())
    loop(0, chunks, lambda k: fold_copy(k).wait_send())

    @pl.when(has_outer)
    def _():
        loop(0, chunks, lambda k: user_copy(k).wait_send())

    loop(0, chunks, lambda k: out_copy(k).wait())
    for j in range(item_tiles):
        panel_out_copy(j).wait()


def finish(users, panel, user_out, panel_out, user_v, panel_v, got, sent):
    pieces = []
    for a, held, b in ((users, user_v, user_out), (panel, panel_v, panel_out)):
        n = a.shape[0] // PIECES
        for i in range(PIECES):
            of = pl.ds(i * n, n)
            at = len(pieces)
            pieces.append((
                pltpu.make_async_copy(a.at[of], held.at[of], got.at[at]),
                pltpu.make_async_copy(held.at[of], b.at[of], sent.at[at])))
    for bring, _ in pieces:
        bring.start()
    for bring, give in pieces:
        bring.wait()
        give.start()
    for _, give in pieces:
        give.wait()


def per_device(
    n_blk, n_split,
    ratings, user_tile, item_tile, tile_count, user_count, item_count, user_factors, item_factors
):
    visits, slots, tile = ratings.shape[1], ratings.shape[3], ratings.shape[-1]
    users, width = user_factors.shape
    part = item_factors.shape[0]
    user_tiles, item_tiles = users // tile, part // tile
    cell_total = user_tiles * item_tiles
    f32 = jnp.float32
    vmem = pl.BlockSpec(memory_space=pltpu.VMEM)
    hbm = pl.BlockSpec(memory_space=pl.ANY)
    smem = pl.BlockSpec(memory_space=pltpu.SMEM)

    lanes = pl.cdiv(slots + cell_total, LANES) * LANES
    held = pl.cdiv(visits, PAD) * PAD
    ch = tile // 2
    chunks = users // ch
    user_gain = step_gain * users / (slots * tile * tile * n_split)
    item_gain = step_gain * part / (slots * tile * tile)
    group, lag, pace = 2, 4, 1
    sizes = (visits, n_blk, n_split, ch, group, lag, pace, user_gain, item_gain)
    dma = pltpu.SemaphoreType.DMA
    shapes = [jax.ShapeDtypeStruct((users, width), f32), jax.ShapeDtypeStruct((part, width), f32)]
    results = pl.pallas_call(
        functools.partial(run_visits, sizes),
        out_shape=shapes,
        in_specs=[smem, vmem, vmem, hbm, vmem, vmem, hbm, hbm],
        out_specs=[hbm, hbm],
        scratch_shapes=[
            pltpu.VMEM((users, width), f32),
            pltpu.VMEM((users, width), f32),
            pltpu.VMEM((users, width), f32),
            pltpu.VMEM((users, width), f32),
            pltpu.VMEM((2, users, width), f32),
            pltpu.VMEM((visits + 1, item_tiles, width + PAD, tile), f32),
            pltpu.VMEM((part, width), jnp.bfloat16),
            pltpu.VMEM((width, part), jnp.bfloat16),
            pltpu.VMEM((width, part), f32),
            pltpu.VMEM((2, slots, tile, tile), ratings.dtype),
            pltpu.VMEM((slots + 1, tile, tile), f32),
            pltpu.VMEM((held, lanes), jnp.int32),
            pltpu.VMEM((held, lanes), jnp.int32),
            pltpu.VMEM((held, lanes), f32),
            pltpu.SMEM((held, lanes), jnp.int32),
            pltpu.SMEM((held, lanes), f32),
            pltpu.VMEM((part, width), f32),
            dma((chunks,)), dma((chunks,)), dma((2, chunks)), dma((chunks,)), dma((chunks,)),
            dma((visits, item_tiles)), dma((visits, item_tiles)), dma((2, PIECES)), dma((2,)),
            dma((2,)), dma((chunks + item_tiles,)),
        ],
        compiler_params=pltpu.CompilerParams(collective_id=0, has_side_effects=True),
        name="run_visits",
    )(
        tile_count.reshape(visits), user_tile.reshape(visits, 1, slots), item_tile.reshape(visits, 1, slots),
        ratings.reshape(visits, slots, tile, tile),
        user_count.reshape(users // tile, tile), item_count.reshape(item_tiles, tile), user_factors, item_factors,
    )
    return pl.pallas_call(
        finish, out_shape=shapes, in_specs=[hbm, hbm], out_specs=[hbm, hbm],
        scratch_shapes=[
            pltpu.VMEM((users, width), f32), pltpu.VMEM((part, width), f32), dma((2 * PIECES,)), dma((2 * PIECES,))],
        name="finish")(*results)


def solution(mesh):
    return jax.shard_map(
        functools.partial(per_device, mesh.shape["blk"], mesh.shape["split"]),
        mesh=mesh,
        in_specs=(
            P("blk", None, "split", None, None, None),
            P("blk", None, "split", None),
            P("blk", None, "split", None),
            P("blk", None, "split"),
            P("blk"),
            P(("blk", "split")),
            P("blk", None),
            P(("blk", "split"), None),
        ),
        out_specs=(P("blk", None), P(("blk", "split"), None)),
        check_vma=False,
    )
```

```python
import functools

import jax
import jax.numpy as jnp
from jax import lax
from jax.experimental import pallas as pl
from jax.experimental.pallas import tpu as pltpu
from jax.sharding import PartitionSpec as P

MESH = pl.DeviceIdType.MESH
step_gain = 12.0
decay_rate = 0.05
PAD = 8
LANES = 128
PIECES = 4
VMEM_LIMIT = 60 << 20


def column(row, width):
    return jnp.broadcast_to(row, (width, row.shape[1])).T


def run_visits(
    sizes, tile_count_in, user_tile_in, item_tile_in, ratings, user_count_in, item_count_in, user_in, panel_in,
    user_out, panel_out,
    u, ustep, g, fold, peer, vp, v16, v16t, gi, tiles, sums, key, chain_v, live_v, chain, live, turn_v,
    tile_count, user_tile, item_tile, user_count, item_count,
    g_sent, fold_got, peer_got, u_sent, u_got, v_sent, v_got, tiles_got, chain_got, in_got,
):
    visits, n_blk, n_split, ch, group, lag, lead, slow, user_gain, item_gain = sizes
    slots, tile = ratings.shape[1], ratings.shape[-1]
    users, width = user_in.shape
    part = panel_in.shape[0]
    item_tiles = part // tile
    chunks = users // ch
    rows_of = group * ch // tile
    cells_of = rows_of * item_tiles
    f32, bf16 = jnp.float32, jnp.bfloat16

    b, s = lax.axis_index("blk"), lax.axis_index("split")
    half = n_split // 2
    left_side = s < half
    inward = jnp.where(left_side, s + 1, s - 1)
    outward = jnp.where(left_side, s - 1, s + 1)
    middle = (s == half - 1) | (s == half)
    has_outer = (s > 0) & (s < n_split - 1)
    back = lax.rem(b + n_blk - 1, n_blk)
    front = lax.rem(b + 1, n_blk)
    home = lax.rem(b + visits - 1, n_blk)
    guest = lax.rem(b + n_blk * visits - (visits - 1), n_blk)

    barrier = pltpu.get_barrier_semaphore()
    for other in (back, front, home, guest):
        pl.semaphore_signal(barrier, inc=1, device_id={"blk": other}, device_id_type=MESH)
    pl.semaphore_signal(barrier, inc=1, device_id={"split": inward}, device_id_type=MESH)

    @pl.when(has_outer)
    def _():
        pl.semaphore_signal(barrier, inc=1, device_id={"split": outward}, device_id_type=MESH)

    def rows(k):
        return pl.ds(pl.multiple_of(k * ch, ch), ch)

    def tiles_copy(v, i):
        slot, of = lax.rem(v, 2), pl.ds(i * slots // PIECES, (i + 1) * slots // PIECES - i * slots // PIECES)
        return pltpu.make_async_copy(ratings.at[v, of], tiles.at[slot, of], tiles_got.at[slot, i])

    def start_tiles(v):
        for i in range(PIECES):
            tiles_copy(v, i).start()

    def add_tiles(v, lo, hi):
        slot = lax.rem(v, 2)

        def add(t, carry):
            sums[t + 1] = tiles[slot, t].astype(f32) + sums[chain[v, t]]
            return carry

        lax.fori_loop(lo, hi, add, 0)

    def fold_copy(k):
        return pltpu.make_async_remote_copy(
            src_ref=g.at[rows(k)], dst_ref=fold.at[rows(k)], send_sem=g_sent.at[k],
            recv_sem=fold_got.at[k], device_id={"split": inward}, device_id_type=MESH)

    def peer_copy(v, k):
        par = lax.rem(v, 2)
        return pltpu.make_async_remote_copy(
            src_ref=g.at[rows(k)], dst_ref=peer.at[par, rows(k)], send_sem=g_sent.at[k],
            recv_sem=peer_got.at[par, k], device_id={"split": inward}, device_id_type=MESH)

    def user_copy(k):
        return pltpu.make_async_remote_copy(
            src_ref=u.at[rows(k)], dst_ref=u.at[rows(k)], send_sem=u_sent.at[k],
            recv_sem=u_got.at[k], device_id={"split": outward}, device_id_type=MESH)

    def panel_copy(v, j, to):
        return pltpu.make_async_remote_copy(
            src_ref=vp.at[v, j], dst_ref=vp.at[v + 1, j], send_sem=v_sent.at[v, j],
            recv_sem=v_got.at[v, j], device_id={"blk": to}, device_id_type=MESH)

    pairs = (
        (tile_count_in, tile_count), (user_tile_in, user_tile), (item_tile_in, item_tile),
        (item_count_in, item_count), (user_count_in, user_count), (panel_in, turn_v), (user_in, u))
    in_copies = [pltpu.make_async_copy(a, to, in_got.at[i]) for i, (a, to) in enumerate(pairs)]
    for copy in in_copies:
        copy.start()
    start_tiles(0)
    if visits > 1:
        start_tiles(1)
    cell_total = users // tile * item_tiles
    lane = lax.broadcasted_iota(jnp.int32, key.shape, 1)
    key[...] = lane - slots
    for copy in in_copies[:3]:
        copy.wait()
    at = lax.broadcasted_iota(jnp.int32, (1, slots), 1)
    for v in range(visits):
        cell = user_tile[v] * item_tiles + item_tile[v]
        key[v:v + 1, :slots] = jnp.where(at < tile_count[v], cell, cell_total)
    turned = key[...].T
    chain_v[...] = jnp.zeros_like(chain_v)
    live_v[...] = jnp.zeros_like(live_v)
    number = lax.broadcasted_iota(jnp.int32, (slots, key.shape[1]), 0)
    ahead = lax.broadcasted_iota(jnp.int32, number.shape, 1)
    ahead = jnp.minimum(ahead, slots)
    for v in range(visits):
        same = turned[:slots, v:v + 1] == key[v:v + 1]
        chain_v[v:v + 1] = jnp.max(
            jnp.where(same & (number < ahead), number + 1, 0), axis=0, keepdims=True)
        live_v[v:v + 1] = jnp.sum(jnp.where(same, 1.0, 0.0), axis=0, keepdims=True)
    chain_copies = [
        pltpu.make_async_copy(chain_v, chain, chain_got.at[0]), pltpu.make_async_copy(live_v, live, chain_got.at[1])]
    for copy in chain_copies:
        copy.start()
    sums[0] = jnp.zeros(sums.shape[1:], f32)
    for copy in in_copies[3:6]:
        copy.wait()
    item_step = item_gain / jnp.sqrt(item_count[...].astype(f32))
    user_step = user_gain / jnp.sqrt(user_count[...].astype(f32))
    for a in range(users // tile):
        ustep[a * tile:(a + 1) * tile] = column(user_step[a:a + 1], width)
    for j in range(item_tiles):
        vp[0, j, :width] = turn_v[j * tile:(j + 1) * tile].T
        vp[0, j, width:] = jnp.broadcast_to(item_step[j:j + 1], (PAD, tile))
    for copy in chain_copies:
        copy.wait()
    for i in range(PIECES):
        tiles_copy(0, i).wait()
        add_tiles(0, i * slots // PIECES, (i + 1) * slots // PIECES)
    in_copies[6].wait()
    pl.semaphore_wait(barrier, jnp.where(has_outer, 6, 5))

    def grads(v, q):
        of = pl.ds(pl.multiple_of(q * group * ch, group * ch), group * ch)
        user_half = u[of].astype(bf16)
        predicted = jnp.dot(user_half, v16t[...], preferred_element_type=f32)
        high, low = [], []
        for a in range(rows_of):
            hs, ls = [], []
            for j in range(item_tiles):
                c = q * cells_of + a * item_tiles + j
                err = sums[chain[v, slots + c]] - live[v, slots + c] * predicted[
                    a * tile:(a + 1) * tile, j * tile:(j + 1) * tile]
                h = err.astype(bf16)
                hs.append(h)
                ls.append((err - h.astype(f32)).astype(bf16))
            high.append(jnp.concatenate(hs, axis=1))
            low.append(jnp.concatenate(ls, axis=1))
        both = jnp.concatenate(high + low, axis=0)
        gu = jnp.dot(both, v16[...], preferred_element_type=f32)
        gu = gu[:group * ch] + gu[group * ch:]
        @pl.when(v > 0)
        def _():
            for k in range(group):
                fold_copy(q * group + k).wait_send()

        g[of] = gu

        @pl.when(jnp.logical_not(has_outer))
        def _():
            for k in range(group):
                send_in(v, q * group + k)

        over = (((0,), (0,)), ((), ()))
        twice = jnp.concatenate([user_half, user_half], axis=0)
        gi[...] += lax.dot_general(twice, both, over, preferred_element_type=f32)

    def send_in(v, k):
        @pl.when(middle)
        def _():
            peer_copy(v, k).start()

        @pl.when(jnp.logical_not(middle))
        def _():
            fold_copy(k).start()

    def pass_in(v, k):
        fold_copy(k).wait_recv()
        g[rows(k)] += fold[rows(k)]
        send_in(v, k)

    def settle(v, k):
        @pl.when(middle)
        def _():
            peer_copy(v, k).wait_recv()

            @pl.when(has_outer & (v > 0))
            def _():
                user_copy(k).wait_send()

            old = u[rows(k)]
            grad = g[rows(k)] + peer[lax.rem(v, 2), rows(k)]
            u[rows(k)] = old + ustep[rows(k)] * (grad - decay_rate * old)

        @pl.when(jnp.logical_not(middle))
        def _():
            @pl.when(has_outer & (v > 0))
            def _():
                user_copy(k).wait_send()

            user_copy(k).wait_recv()

        @pl.when(has_outer)
        def _():
            user_copy(k).start()

        @pl.when(v == visits - 1)
        def _():
            user_out[rows(k)] = u[rows(k)]

    def loop(lo, hi, step):
        def body(k, carry):
            step(k)
            return carry

        lax.fori_loop(lo, hi, body, 0)

    groups = chunks // group
    turned = 2 * (groups - 1) - slow
    rest = chunks - turned

    def step(i):
        @pl.when((i >= 0) & (i < visits * chunks))
        def _():
            pass_in(i // chunks, i % chunks)

        @pl.when(i >= lag)
        def _():
            settle((i - lag) // chunks, (i - lag) % chunks)

    def visit(v, carry):
        for j in range(item_tiles):
            @pl.when(v > 0)
            def _():
                panel_copy(v - 1, j, back).wait_recv()

            at = slice(j * tile, (j + 1) * tile)
            items = vp[v, j, :width]
            v16t[:, at] = items.astype(bf16)
            v16[at] = items.T.astype(bf16)

        gi[...] = jnp.zeros_like(gi)

        def turn(q):
            @pl.when(jnp.logical_not(has_outer) & (v > 0))
            def _():
                for k in range(group):
                    settle(v - 1, q * group + k)

            grads(v, q)

            @pl.when(has_outer & (q < groups - 1))
            def _():
                at = v * chunks - lead + q + jnp.maximum(q - slow, 0)
                step(at)

                @pl.when(q >= slow)
                def _():
                    step(at + 1)

        loop(0, groups, turn)
        for j in range(item_tiles):
            at = slice(j * tile, (j + 1) * tile)
            old = vp[v, j, :width]
            vp[v, j, :width] = old + vp[v, j, width:width + 1] * (gi[:, at] - decay_rate * old)

            @pl.when(v < visits - 1)
            def _():
                panel_copy(v, j, back).start()

            @pl.when(v == visits - 1)
            def _():
                panel_copy(v, j, home).start()

        @pl.when(v + 1 < visits)
        def _():
            for i in range(PIECES):
                tiles_copy(v + 1, i).wait()

        @pl.when(v + 2 < visits)
        def _():
            start_tiles(v + 2)

        @pl.when(has_outer)
        def _():
            def early(k):
                step(v * chunks - lead + turned + k)

                @pl.when(v + 1 < visits)
                def _():
                    add_tiles(v + 1, k * slots // rest, (k + 1) * slots // rest)

            loop(0, rest, early)

        @pl.when(jnp.logical_not(has_outer))
        def _():
            @pl.when(v + 1 < visits)
            def _():
                add_tiles(v + 1, 0, slots)

        return carry

    lax.fori_loop(0, visits, visit, 0)

    @pl.when(has_outer)
    def _():
        loop(visits * chunks - lead, visits * chunks, step)

    @pl.when(jnp.logical_not(has_outer))
    def _():
        loop(0, chunks - group, lambda k: settle(visits - 1, k))

    for j in range(item_tiles):
        panel_copy(visits - 1, j, home).wait_recv()
        panel_out[j * tile:(j + 1) * tile] = vp[visits, j, :width].T

    @pl.when(has_outer)
    def _():
        loop(visits * chunks, visits * chunks + lag, step)

    @pl.when(jnp.logical_not(has_outer))
    def _():
        loop(chunks - group, chunks, lambda k: settle(visits - 1, k))

    for j in range(item_tiles):
        loop(0, visits, lambda v: panel_copy(v, j, back).wait_send())
    loop(0, chunks, lambda k: fold_copy(k).wait_send())

    @pl.when(has_outer)
    def _():
        loop(0, chunks, lambda k: user_copy(k).wait_send())


def per_device(
    n_blk, n_split,
    ratings, user_tile, item_tile, tile_count, user_count, item_count, user_factors, item_factors
):
    visits, slots, tile = ratings.shape[1], ratings.shape[3], ratings.shape[-1]
    users, width = user_factors.shape
    part = item_factors.shape[0]
    user_tiles, item_tiles = users // tile, part // tile
    cell_total = user_tiles * item_tiles
    f32 = jnp.float32
    vmem = pl.BlockSpec(memory_space=pltpu.VMEM)
    hbm = pl.BlockSpec(memory_space=pl.ANY)

    lanes = pl.cdiv(slots + cell_total, LANES) * LANES
    held = pl.cdiv(visits, PAD) * PAD
    ch = tile // 2
    chunks = users // ch
    user_gain = step_gain * users / (slots * tile * tile * n_split)
    item_gain = step_gain * part / (slots * tile * tile)
    group, lag, lead, slow = 2, 4, 3, 7
    sizes = (visits, n_blk, n_split, ch, group, lag, lead, slow, user_gain, item_gain)
    dma = pltpu.SemaphoreType.DMA
    shapes = [jax.ShapeDtypeStruct((users, width), f32), jax.ShapeDtypeStruct((part, width), f32)]
    return pl.pallas_call(
        functools.partial(run_visits, sizes),
        out_shape=[pltpu.VMEM(x.shape, x.dtype) for x in shapes],
        in_specs=[hbm] * 8,
        out_specs=[vmem, vmem],
        scratch_shapes=[
            pltpu.VMEM((users, width), f32),
            pltpu.VMEM((users, width), f32),
            pltpu.VMEM((users, width), f32),
            pltpu.VMEM((users, width), f32),
            pltpu.VMEM((2, users, width), f32),
            pltpu.VMEM((visits + 1, item_tiles, width + PAD, tile), f32),
            pltpu.VMEM((part, width), jnp.bfloat16),
            pltpu.VMEM((width, part), jnp.bfloat16),
            pltpu.VMEM((width, part), f32),
            pltpu.VMEM((2, slots, tile, tile), ratings.dtype),
            pltpu.VMEM((slots + 1, tile, tile), f32),
            pltpu.VMEM((held, lanes), jnp.int32),
            pltpu.VMEM((held, lanes), jnp.int32),
            pltpu.VMEM((held, lanes), f32),
            pltpu.SMEM((held, lanes), jnp.int32),
            pltpu.SMEM((held, lanes), f32),
            pltpu.VMEM((part, width), f32),
            pltpu.SMEM((visits,), jnp.int32),
            pltpu.VMEM((visits, 1, slots), jnp.int32),
            pltpu.VMEM((visits, 1, slots), jnp.int32),
            pltpu.VMEM((users // tile, tile), jnp.int32),
            pltpu.VMEM((item_tiles, tile), jnp.int32),
            dma((chunks,)), dma((chunks,)), dma((2, chunks)), dma((chunks,)), dma((chunks,)),
            dma((visits, item_tiles)), dma((visits, item_tiles)), dma((2, PIECES)), dma((2,)),
            dma((7,)),
        ],
        compiler_params=pltpu.CompilerParams(collective_id=0, has_side_effects=True, vmem_limit_bytes=VMEM_LIMIT),
        name="run_visits",
    )(
        tile_count.reshape(visits), user_tile.reshape(visits, 1, slots), item_tile.reshape(visits, 1, slots),
        ratings.reshape(visits, slots, tile, tile),
        user_count.reshape(users // tile, tile), item_count.reshape(item_tiles, tile), user_factors, item_factors,
    )


def solution(mesh):
    return jax.shard_map(
        functools.partial(per_device, mesh.shape["blk"], mesh.shape["split"]),
        mesh=mesh,
        in_specs=(
            P("blk", None, "split", None, None, None),
            P("blk", None, "split", None),
            P("blk", None, "split", None),
            P("blk", None, "split"),
            P("blk"),
            P(("blk", "split")),
            P("blk", None),
            P(("blk", "split"), None),
        ),
        out_specs=(P("blk", None), P(("blk", "split"), None)),
        check_vma=False,
    )
```

```python
import functools

import jax
import jax.numpy as jnp
from jax import lax
from jax.experimental import pallas as pl
from jax.experimental.pallas import tpu as pltpu
from jax.sharding import PartitionSpec as P

MESH = pl.DeviceIdType.MESH
step_gain = 12.0
decay_rate = 0.05
PAD = 8
LANES = 128
PIECES = 4
VMEM_LIMIT = 60 << 20


def column(row, width):
    return jnp.broadcast_to(row, (width, row.shape[1])).T


def run_visits(
    sizes, tile_count_in, user_tile_in, item_tile_in, ratings, user_count_in, item_count_in, user_in, panel_in,
    user_out, panel_out,
    u, ustep, g, fold, peer, vp, v16, v16t, gi, tiles, sums, key, chain_v, live_v, chain, live, turn_v,
    tile_count, user_tile, item_tile, user_count, item_count,
    g_sent, fold_got, peer_got, u_sent, u_got, v_sent, v_got, tiles_got, chain_got, in_got,
):
    visits, n_blk, n_split, ch, group, lag, lead, slow, user_gain, item_gain = sizes
    slots, tile = ratings.shape[1], ratings.shape[-1]
    users, width = user_in.shape
    part = panel_in.shape[0]
    item_tiles = part // tile
    chunks = users // ch
    rows_of = group * ch // tile
    cells_of = rows_of * item_tiles
    f32, bf16 = jnp.float32, jnp.bfloat16

    b, s = lax.axis_index("blk"), lax.axis_index("split")
    half = n_split // 2
    left_side = s < half
    inward = jnp.where(left_side, s + 1, s - 1)
    outward = jnp.where(left_side, s - 1, s + 1)
    middle = (s == half - 1) | (s == half)
    has_outer = (s > 0) & (s < n_split - 1)
    back = lax.rem(b + n_blk - 1, n_blk)
    front = lax.rem(b + 1, n_blk)
    home = lax.rem(b + visits - 1, n_blk)
    guest = lax.rem(b + n_blk * visits - (visits - 1), n_blk)

    barrier = pltpu.get_barrier_semaphore()
    for other in (back, front, home, guest):
        pl.semaphore_signal(barrier, inc=1, device_id={"blk": other}, device_id_type=MESH)
    pl.semaphore_signal(barrier, inc=1, device_id={"split": inward}, device_id_type=MESH)

    @pl.when(has_outer)
    def _():
        pl.semaphore_signal(barrier, inc=1, device_id={"split": outward}, device_id_type=MESH)

    def rows(k):
        return pl.ds(pl.multiple_of(k * ch, ch), ch)

    def tiles_copy(v, i):
        slot, of = lax.rem(v, 2), pl.ds(i * slots // PIECES, (i + 1) * slots // PIECES - i * slots // PIECES)
        return pltpu.make_async_copy(ratings.at[v, of], tiles.at[slot, of], tiles_got.at[slot, i])

    def start_tiles(v):
        for i in range(PIECES):
            tiles_copy(v, i).start()

    def add_tiles(v, lo, hi):
        slot = lax.rem(v, 2)

        def add(t, carry):
            sums[t + 1] = tiles[slot, t].astype(f32) + sums[chain[v, t]]
            return carry

        lax.fori_loop(lo, hi, add, 0)

    def fold_copy(k):
        return pltpu.make_async_remote_copy(
            src_ref=g.at[rows(k)], dst_ref=fold.at[rows(k)], send_sem=g_sent.at[k],
            recv_sem=fold_got.at[k], device_id={"split": inward}, device_id_type=MESH)

    def peer_copy(v, k):
        par = lax.rem(v, 2)
        return pltpu.make_async_remote_copy(
            src_ref=g.at[rows(k)], dst_ref=peer.at[par, rows(k)], send_sem=g_sent.at[k],
            recv_sem=peer_got.at[par, k], device_id={"split": inward}, device_id_type=MESH)

    def user_copy(k):
        return pltpu.make_async_remote_copy(
            src_ref=u.at[rows(k)], dst_ref=u.at[rows(k)], send_sem=u_sent.at[k],
            recv_sem=u_got.at[k], device_id={"split": outward}, device_id_type=MESH)

    def panel_copy(v, j, to):
        return pltpu.make_async_remote_copy(
            src_ref=vp.at[v, j], dst_ref=vp.at[v + 1, j], send_sem=v_sent.at[v, j],
            recv_sem=v_got.at[v, j], device_id={"blk": to}, device_id_type=MESH)

    pairs = (
        (tile_count_in, tile_count), (user_tile_in, user_tile), (item_tile_in, item_tile),
        (item_count_in, item_count), (user_count_in, user_count), (panel_in, turn_v), (user_in, u))
    in_copies = [pltpu.make_async_copy(a, to, in_got.at[i]) for i, (a, to) in enumerate(pairs)]
    for copy in in_copies:
        copy.start()
    start_tiles(0)
    if visits > 1:
        start_tiles(1)
    cell_total = users // tile * item_tiles
    lane = lax.broadcasted_iota(jnp.int32, key.shape, 1)
    key[...] = lane - slots
    for copy in in_copies[:3]:
        copy.wait()
    at = lax.broadcasted_iota(jnp.int32, (1, slots), 1)
    for v in range(visits):
        cell = user_tile[v] * item_tiles + item_tile[v]
        key[v:v + 1, :slots] = jnp.where(at < tile_count[v], cell, cell_total)
    turned = key[...].T
    chain_v[...] = jnp.zeros_like(chain_v)
    live_v[...] = jnp.zeros_like(live_v)
    number = lax.broadcasted_iota(jnp.int32, (slots, key.shape[1]), 0)
    ahead = lax.broadcasted_iota(jnp.int32, number.shape, 1)
    ahead = jnp.minimum(ahead, slots)
    for v in range(visits):
        same = turned[:slots, v:v + 1] == key[v:v + 1]
        chain_v[v:v + 1] = jnp.max(
            jnp.where(same & (number < ahead), number + 1, 0), axis=0, keepdims=True)
        live_v[v:v + 1] = jnp.sum(jnp.where(same, 1.0, 0.0), axis=0, keepdims=True)
    chain_copies = [
        pltpu.make_async_copy(chain_v, chain, chain_got.at[0]), pltpu.make_async_copy(live_v, live, chain_got.at[1])]
    for copy in chain_copies:
        copy.start()
    sums[0] = jnp.zeros(sums.shape[1:], f32)
    for copy in in_copies[3:6]:
        copy.wait()
    item_step = item_gain / jnp.sqrt(item_count[...].astype(f32))
    user_step = user_gain / jnp.sqrt(user_count[...].astype(f32))
    for a in range(users // tile):
        ustep[a * tile:(a + 1) * tile] = column(user_step[a:a + 1], width)
    for j in range(item_tiles):
        vp[0, j, :width] = turn_v[j * tile:(j + 1) * tile].T
        vp[0, j, width:] = jnp.broadcast_to(item_step[j:j + 1], (PAD, tile))
    for copy in chain_copies:
        copy.wait()
    for i in range(PIECES):
        tiles_copy(0, i).wait()
        add_tiles(0, i * slots // PIECES, (i + 1) * slots // PIECES)
    in_copies[6].wait()
    pl.semaphore_wait(barrier, jnp.where(has_outer, 6, 5))

    def grads(v, q):
        of = pl.ds(pl.multiple_of(q * group * ch, group * ch), group * ch)
        user_half = u[of].astype(bf16)
        predicted = jnp.dot(user_half, v16t[...], preferred_element_type=f32)
        high, low = [], []
        for a in range(rows_of):
            hs, ls = [], []
            for j in range(item_tiles):
                c = q * cells_of + a * item_tiles + j
                err = sums[chain[v, slots + c]] - live[v, slots + c] * predicted[
                    a * tile:(a + 1) * tile, j * tile:(j + 1) * tile]
                h = err.astype(bf16)
                hs.append(h)
                ls.append((err - h.astype(f32)).astype(bf16))
            high.append(jnp.concatenate(hs, axis=1))
            low.append(jnp.concatenate(ls, axis=1))
        both = jnp.concatenate(high + low, axis=0)
        gu = jnp.dot(both, v16[...], preferred_element_type=f32)
        gu = gu[:group * ch] + gu[group * ch:]
        @pl.when(v > 0)
        def _():
            for k in range(group):
                fold_copy(q * group + k).wait_send()

        g[of] = gu

        @pl.when(jnp.logical_not(has_outer))
        def _():
            for k in range(group):
                send_in(v, q * group + k)

        over = (((0,), (0,)), ((), ()))
        twice = jnp.concatenate([user_half, user_half], axis=0)
        gi[...] += lax.dot_general(twice, both, over, preferred_element_type=f32)

    def send_in(v, k):
        @pl.when(middle)
        def _():
            peer_copy(v, k).start()

        @pl.when(jnp.logical_not(middle))
        def _():
            fold_copy(k).start()

    def pass_in(v, k):
        fold_copy(k).wait_recv()
        g[rows(k)] += fold[rows(k)]
        send_in(v, k)

    def settle(v, k):
        @pl.when(middle)
        def _():
            peer_copy(v, k).wait_recv()

            @pl.when(has_outer & (v > 0))
            def _():
                user_copy(k).wait_send()

            old = u[rows(k)]
            grad = g[rows(k)] + peer[lax.rem(v, 2), rows(k)]
            u[rows(k)] = old + ustep[rows(k)] * (grad - decay_rate * old)

        @pl.when(jnp.logical_not(middle))
        def _():
            @pl.when(has_outer & (v > 0))
            def _():
                user_copy(k).wait_send()

            user_copy(k).wait_recv()

        @pl.when(has_outer)
        def _():
            user_copy(k).start()

        @pl.when(v == visits - 1)
        def _():
            user_out[rows(k)] = u[rows(k)]

    def loop(lo, hi, step):
        def body(k, carry):
            step(k)
            return carry

        lax.fori_loop(lo, hi, body, 0)

    groups = chunks // group
    turned = 2 * (groups - 1) - slow
    rest = chunks - turned

    def step(i):
        @pl.when((i >= 0) & (i < visits * chunks))
        def _():
            pass_in(i // chunks, i % chunks)

        @pl.when(i >= lag)
        def _():
            settle((i - lag) // chunks, (i - lag) % chunks)

    def visit(v, carry):
        for j in range(item_tiles):
            @pl.when(v > 0)
            def _():
                panel_copy(v - 1, j, back).wait_recv()

            at = slice(j * tile, (j + 1) * tile)
            items = vp[v, j, :width]
            v16t[:, at] = items.astype(bf16)
            v16[at] = items.astype(bf16).T

        gi[...] = jnp.zeros_like(gi)

        def turn(q):
            @pl.when(jnp.logical_not(has_outer) & (v > 0))
            def _():
                for k in range(group):
                    settle(v - 1, q * group + k)

            grads(v, q)

            @pl.when(has_outer & (q < groups - 1))
            def _():
                at = v * chunks - lead + q + jnp.maximum(q - slow, 0)
                step(at)

                @pl.when(q >= slow)
                def _():
                    step(at + 1)

        loop(0, groups, turn)
        for j in range(item_tiles):
            at = slice(j * tile, (j + 1) * tile)
            old = vp[v, j, :width]
            vp[v, j, :width] = old + vp[v, j, width:width + 1] * (gi[:, at] - decay_rate * old)

            @pl.when(v < visits - 1)
            def _():
                panel_copy(v, j, back).start()

            @pl.when(v == visits - 1)
            def _():
                panel_copy(v, j, home).start()

        @pl.when(v + 1 < visits)
        def _():
            for i in range(PIECES):
                tiles_copy(v + 1, i).wait()

        @pl.when(v + 2 < visits)
        def _():
            start_tiles(v + 2)

        @pl.when(has_outer)
        def _():
            def early(k):
                step(v * chunks - lead + turned + k)

                @pl.when(v + 1 < visits)
                def _():
                    add_tiles(v + 1, k * slots // rest, (k + 1) * slots // rest)

            loop(0, rest, early)

        @pl.when(jnp.logical_not(has_outer))
        def _():
            @pl.when(v + 1 < visits)
            def _():
                add_tiles(v + 1, 0, slots)

        return carry

    lax.fori_loop(0, visits, visit, 0)

    @pl.when(has_outer)
    def _():
        loop(visits * chunks - lead, visits * chunks, step)

    @pl.when(jnp.logical_not(has_outer))
    def _():
        loop(0, chunks - group, lambda k: settle(visits - 1, k))

    for j in range(item_tiles):
        panel_copy(visits - 1, j, home).wait_recv()
        panel_out[j * tile:(j + 1) * tile] = vp[visits, j, :width].T

    @pl.when(has_outer)
    def _():
        loop(visits * chunks, visits * chunks + lag, step)

    @pl.when(jnp.logical_not(has_outer))
    def _():
        loop(chunks - group, chunks, lambda k: settle(visits - 1, k))

    for j in range(item_tiles):
        loop(0, visits, lambda v: panel_copy(v, j, back).wait_send())
    loop(0, chunks, lambda k: fold_copy(k).wait_send())

    @pl.when(has_outer)
    def _():
        loop(0, chunks, lambda k: user_copy(k).wait_send())


def finish(users, panel, user_out, panel_out, sent):
    copies = [
        pltpu.make_async_copy(users, user_out, sent.at[0]), pltpu.make_async_copy(panel, panel_out, sent.at[1])]
    for copy in copies:
        copy.start()
    for copy in copies:
        copy.wait()


def per_device(
    n_blk, n_split,
    ratings, user_tile, item_tile, tile_count, user_count, item_count, user_factors, item_factors
):
    visits, slots, tile = ratings.shape[1], ratings.shape[3], ratings.shape[-1]
    users, width = user_factors.shape
    part = item_factors.shape[0]
    user_tiles, item_tiles = users // tile, part // tile
    cell_total = user_tiles * item_tiles
    f32 = jnp.float32
    vmem = pl.BlockSpec(memory_space=pltpu.VMEM)
    hbm = pl.BlockSpec(memory_space=pl.ANY)

    lanes = pl.cdiv(slots + cell_total, LANES) * LANES
    held = pl.cdiv(visits, PAD) * PAD
    ch = tile // 2
    chunks = users // ch
    user_gain = step_gain * users / (slots * tile * tile * n_split)
    item_gain = step_gain * part / (slots * tile * tile)
    group, lag, lead, slow = 2, 4, 3, 7
    sizes = (visits, n_blk, n_split, ch, group, lag, lead, slow, user_gain, item_gain)
    dma = pltpu.SemaphoreType.DMA
    shapes = [jax.ShapeDtypeStruct((users, width), f32), jax.ShapeDtypeStruct((part, width), f32)]
    results = pl.pallas_call(
        functools.partial(run_visits, sizes),
        out_shape=[pltpu.VMEM(x.shape, x.dtype) for x in shapes],
        in_specs=[hbm] * 8,
        out_specs=[vmem, vmem],
        scratch_shapes=[
            pltpu.VMEM((users, width), f32),
            pltpu.VMEM((users, width), f32),
            pltpu.VMEM((users, width), f32),
            pltpu.VMEM((users, width), f32),
            pltpu.VMEM((2, users, width), f32),
            pltpu.VMEM((visits + 1, item_tiles, width + PAD, tile), f32),
            pltpu.VMEM((part, width), jnp.bfloat16),
            pltpu.VMEM((width, part), jnp.bfloat16),
            pltpu.VMEM((width, part), f32),
            pltpu.VMEM((2, slots, tile, tile), ratings.dtype),
            pltpu.VMEM((slots + 1, tile, tile), f32),
            pltpu.VMEM((held, lanes), jnp.int32),
            pltpu.VMEM((held, lanes), jnp.int32),
            pltpu.VMEM((held, lanes), f32),
            pltpu.SMEM((held, lanes), jnp.int32),
            pltpu.SMEM((held, lanes), f32),
            pltpu.VMEM((part, width), f32),
            pltpu.SMEM((visits,), jnp.int32),
            pltpu.VMEM((visits, 1, slots), jnp.int32),
            pltpu.VMEM((visits, 1, slots), jnp.int32),
            pltpu.VMEM((users // tile, tile), jnp.int32),
            pltpu.VMEM((item_tiles, tile), jnp.int32),
            dma((chunks,)), dma((chunks,)), dma((2, chunks)), dma((chunks,)), dma((chunks,)),
            dma((visits, item_tiles)), dma((visits, item_tiles)), dma((2, PIECES)), dma((2,)),
            dma((7,)),
        ],
        compiler_params=pltpu.CompilerParams(collective_id=0, has_side_effects=True, vmem_limit_bytes=VMEM_LIMIT),
        name="run_visits",
    )(
        tile_count.reshape(visits), user_tile.reshape(visits, 1, slots), item_tile.reshape(visits, 1, slots),
        ratings.reshape(visits, slots, tile, tile),
        user_count.reshape(users // tile, tile), item_count.reshape(item_tiles, tile), user_factors, item_factors,
    )
    return pl.pallas_call(
        finish, out_shape=shapes, in_specs=[vmem, vmem], out_specs=[hbm, hbm],
        scratch_shapes=[dma((2,))], name="finish",
    )(*(pltpu.with_memory_space_constraint(x, pltpu.VMEM) for x in results))


def solution(mesh):
    return jax.shard_map(
        functools.partial(per_device, mesh.shape["blk"], mesh.shape["split"]),
        mesh=mesh,
        in_specs=(
            P("blk", None, "split", None, None, None),
            P("blk", None, "split", None),
            P("blk", None, "split", None),
            P("blk", None, "split"),
            P("blk"),
            P(("blk", "split")),
            P("blk", None),
            P(("blk", "split"), None),
        ),
        out_specs=(P("blk", None), P(("blk", "split"), None)),
        check_vma=False,
    )
```

```python
import functools

import jax
import jax.numpy as jnp
from jax import lax
from jax.experimental import pallas as pl
from jax.experimental.pallas import tpu as pltpu
from jax.sharding import PartitionSpec as P

MESH = pl.DeviceIdType.MESH
step_gain = 12.0
decay_rate = 0.05
PAD = 8
LANES = 128
PIECES = 4
VMEM_LIMIT = 60 << 20


def column(row, width):
    return jnp.broadcast_to(row, (width, row.shape[1])).T


def run_visits(
    sizes, tile_count_in, user_tile_in, item_tile_in, ratings, user_count_in, item_count_in, user_in, panel_in,
    user_out, panel_out,
    u, ustep, g, fold, peer, vp, v16, v16t, gi, tiles, sums, key, chain_v, live_v, chain, live, turn_v,
    tile_count, user_tile, item_tile, user_count, item_count,
    g_sent, fold_got, peer_got, u_sent, u_got, v_sent, v_got, tiles_got, chain_got, in_got,
):
    visits, n_blk, n_split, ch, group, lag, lead, slow, user_gain, item_gain = sizes
    slots, tile = ratings.shape[1], ratings.shape[-1]
    users, width = user_in.shape
    part = panel_in.shape[0]
    item_tiles = part // tile
    chunks = users // ch
    rows_of = group * ch // tile
    cells_of = rows_of * item_tiles
    f32, bf16 = jnp.float32, jnp.bfloat16

    b, s = lax.axis_index("blk"), lax.axis_index("split")
    half = n_split // 2
    left_side = s < half
    inward = jnp.where(left_side, s + 1, s - 1)
    outward = jnp.where(left_side, s - 1, s + 1)
    middle = (s == half - 1) | (s == half)
    has_outer = (s > 0) & (s < n_split - 1)
    back = lax.rem(b + n_blk - 1, n_blk)
    front = lax.rem(b + 1, n_blk)
    home = lax.rem(b + visits - 1, n_blk)
    guest = lax.rem(b + n_blk * visits - (visits - 1), n_blk)

    barrier = pltpu.get_barrier_semaphore()
    for other in (back, front, home, guest):
        pl.semaphore_signal(barrier, inc=1, device_id={"blk": other}, device_id_type=MESH)
    pl.semaphore_signal(barrier, inc=1, device_id={"split": inward}, device_id_type=MESH)

    @pl.when(has_outer)
    def _():
        pl.semaphore_signal(barrier, inc=1, device_id={"split": outward}, device_id_type=MESH)

    def rows(k):
        return pl.ds(pl.multiple_of(k * ch, ch), ch)

    def tiles_copy(v, i):
        slot, of = lax.rem(v, 2), pl.ds(i * slots // PIECES, (i + 1) * slots // PIECES - i * slots // PIECES)
        return pltpu.make_async_copy(ratings.at[v, of], tiles.at[slot, of], tiles_got.at[slot, i])

    def start_tiles(v):
        for i in range(PIECES):
            tiles_copy(v, i).start()

    def add_tiles(v, lo, hi):
        slot = lax.rem(v, 2)

        def add(t, carry):
            sums[t + 1] = tiles[slot, t].astype(f32) + sums[chain[v, t]]
            return carry

        lax.fori_loop(lo, hi, add, 0)

    def fold_copy(k):
        return pltpu.make_async_remote_copy(
            src_ref=g.at[rows(k)], dst_ref=fold.at[rows(k)], send_sem=g_sent.at[k],
            recv_sem=fold_got.at[k], device_id={"split": inward}, device_id_type=MESH)

    def peer_copy(v, k):
        par = lax.rem(v, 2)
        return pltpu.make_async_remote_copy(
            src_ref=g.at[rows(k)], dst_ref=peer.at[par, rows(k)], send_sem=g_sent.at[k],
            recv_sem=peer_got.at[par, k], device_id={"split": inward}, device_id_type=MESH)

    def user_copy(k):
        return pltpu.make_async_remote_copy(
            src_ref=u.at[rows(k)], dst_ref=u.at[rows(k)], send_sem=u_sent.at[k],
            recv_sem=u_got.at[k], device_id={"split": outward}, device_id_type=MESH)

    def panel_copy(v, j, to):
        return pltpu.make_async_remote_copy(
            src_ref=vp.at[v, j], dst_ref=vp.at[v + 1, j], send_sem=v_sent.at[v, j],
            recv_sem=v_got.at[v, j], device_id={"blk": to}, device_id_type=MESH)

    pairs = (
        (tile_count_in, tile_count), (user_tile_in, user_tile), (item_tile_in, item_tile),
        (item_count_in, item_count), (user_count_in, user_count), (panel_in, turn_v), (user_in, u))
    in_copies = [pltpu.make_async_copy(a, to, in_got.at[i]) for i, (a, to) in enumerate(pairs)]
    for copy in in_copies:
        copy.start()
    start_tiles(0)
    if visits > 1:
        start_tiles(1)
    cell_total = users // tile * item_tiles
    lane = lax.broadcasted_iota(jnp.int32, key.shape, 1)
    key[...] = lane - slots
    for copy in in_copies[:3]:
        copy.wait()
    at = lax.broadcasted_iota(jnp.int32, (1, slots), 1)
    for v in range(visits):
        cell = user_tile[v] * item_tiles + item_tile[v]
        key[v:v + 1, :slots] = jnp.where(at < tile_count[v], cell, cell_total)
    turned = key[...].T
    chain_v[...] = jnp.zeros_like(chain_v)
    live_v[...] = jnp.zeros_like(live_v)
    number = lax.broadcasted_iota(jnp.int32, (slots, key.shape[1]), 0)
    ahead = lax.broadcasted_iota(jnp.int32, number.shape, 1)
    ahead = jnp.minimum(ahead, slots)
    for v in range(visits):
        same = turned[:slots, v:v + 1] == key[v:v + 1]
        chain_v[v:v + 1] = jnp.max(
            jnp.where(same & (number < ahead), number + 1, 0), axis=0, keepdims=True)
        live_v[v:v + 1] = jnp.sum(jnp.where(same, 1.0, 0.0), axis=0, keepdims=True)
    chain_copies = [
        pltpu.make_async_copy(chain_v, chain, chain_got.at[0]), pltpu.make_async_copy(live_v, live, chain_got.at[1])]
    for copy in chain_copies:
        copy.start()
    sums[0] = jnp.zeros(sums.shape[1:], f32)
    for copy in in_copies[3:6]:
        copy.wait()
    item_step = item_gain / jnp.sqrt(item_count[...].astype(f32))
    user_step = user_gain / jnp.sqrt(user_count[...].astype(f32))
    for a in range(users // tile):
        ustep[a * tile:(a + 1) * tile] = column(user_step[a:a + 1], width)
    for j in range(item_tiles):
        vp[0, j, :width] = turn_v[j * tile:(j + 1) * tile].T
        vp[0, j, width:] = jnp.broadcast_to(item_step[j:j + 1], (PAD, tile))
    for copy in chain_copies:
        copy.wait()
    for i in range(PIECES):
        tiles_copy(0, i).wait()
        add_tiles(0, i * slots // PIECES, (i + 1) * slots // PIECES)
    in_copies[6].wait()
    pl.semaphore_wait(barrier, jnp.where(has_outer, 6, 5))

    def grads(v, q):
        of = pl.ds(pl.multiple_of(q * group * ch, group * ch), group * ch)
        user_half = u[of].astype(bf16)
        predicted = jnp.dot(user_half, v16t[...], preferred_element_type=f32)
        high, low = [], []
        for a in range(rows_of):
            hs, ls = [], []
            for j in range(item_tiles):
                c = q * cells_of + a * item_tiles + j
                err = sums[chain[v, slots + c]] - live[v, slots + c] * predicted[
                    a * tile:(a + 1) * tile, j * tile:(j + 1) * tile]
                h = err.astype(bf16)
                hs.append(h)
                ls.append((err - h.astype(f32)).astype(bf16))
            high.append(jnp.concatenate(hs, axis=1))
            low.append(jnp.concatenate(ls, axis=1))
        both = jnp.concatenate(high + low, axis=0)
        gu = jnp.dot(both, v16[...], preferred_element_type=f32)
        gu = gu[:group * ch] + gu[group * ch:]
        @pl.when(v > 0)
        def _():
            for k in range(group):
                fold_copy(q * group + k).wait_send()

        g[of] = gu

        @pl.when(jnp.logical_not(has_outer))
        def _():
            for k in range(group):
                send_in(v, q * group + k, False)

        over = (((0,), (0,)), ((), ()))
        twice = jnp.concatenate([user_half, user_half], axis=0)
        gi[...] += lax.dot_general(twice, both, over, preferred_element_type=f32)

    def send_in(v, k, inner):
        @choose(middle, known_middle(inner))
        def _():
            peer_copy(v, k).start()

        @choose(jnp.logical_not(middle), negated(known_middle(inner)))
        def _():
            fold_copy(k).start()

    def known_middle(inner):
        return inner if n_split == 4 else None

    def negated(known):
        return None if known is None else not known

    def choose(cond, known):
        def run(body):
            if known is None:
                pl.when(cond)(body)
            elif known:
                body()

        return run

    def pass_in(v, k):
        fold_copy(k).wait_recv()
        g[rows(k)] += fold[rows(k)]
        send_in(v, k, True)

    def settle(v, k, inner):
        if inner:
            @pl.when(v > 0)
            def _():
                user_copy(k).wait_send()

        @choose(middle, known_middle(inner))
        def _():
            peer_copy(v, k).wait_recv()
            old = u[rows(k)]
            grad = g[rows(k)] + peer[lax.rem(v, 2), rows(k)]
            u[rows(k)] = old + ustep[rows(k)] * (grad - decay_rate * old)

        @choose(jnp.logical_not(middle), negated(known_middle(inner)))
        def _():
            user_copy(k).wait_recv()

        if inner:
            user_copy(k).start()

        @pl.when(v == visits - 1)
        def _():
            user_out[rows(k)] = u[rows(k)]

    def loop(lo, hi, step):
        def body(k, carry):
            step(k)
            return carry

        lax.fori_loop(lo, hi, body, 0)

    groups = chunks // group
    turned = 2 * (groups - 1) - slow
    rest = chunks - turned

    def step(i):
        @pl.when((i >= 0) & (i < visits * chunks))
        def _():
            pass_in(i // chunks, i % chunks)

        @pl.when(i >= lag)
        def _():
            settle((i - lag) // chunks, (i - lag) % chunks, True)

    def visit(v, carry):
        gi[...] = jnp.zeros_like(gi)
        for j in range(item_tiles):
            @pl.when(v > 0)
            def _():
                panel_copy(v - 1, j, back).wait_recv()

            at = slice(j * tile, (j + 1) * tile)
            items = vp[v, j, :width]
            v16t[:, at] = items.astype(bf16)
            v16[at] = items.astype(bf16).T

        def turn(q):
            @pl.when(jnp.logical_not(has_outer) & (v > 0))
            def _():
                for k in range(group):
                    settle(v - 1, q * group + k, False)

            grads(v, q)

            @pl.when(has_outer & (q < groups - 1))
            def _():
                at = v * chunks - lead + q + jnp.maximum(q - slow, 0)
                step(at)

                @pl.when(q >= slow)
                def _():
                    step(at + 1)

        loop(0, groups, turn)
        for j in range(item_tiles):
            at = slice(j * tile, (j + 1) * tile)
            old = vp[v, j, :width]
            vp[v, j, :width] = old + vp[v, j, width:width + 1] * (gi[:, at] - decay_rate * old)

            @pl.when(v < visits - 1)
            def _():
                panel_copy(v, j, back).start()

            @pl.when(v == visits - 1)
            def _():
                panel_copy(v, j, home).start()

        @pl.when(v + 1 < visits)
        def _():
            for i in range(PIECES):
                tiles_copy(v + 1, i).wait()

        @pl.when(v + 2 < visits)
        def _():
            start_tiles(v + 2)

        @pl.when(has_outer)
        def _():
            def early(k):
                step(v * chunks - lead + turned + k)

                @pl.when(v + 1 < visits)
                def _():
                    add_tiles(v + 1, k * slots // rest, (k + 1) * slots // rest)

            loop(0, rest, early)

        @pl.when(jnp.logical_not(has_outer))
        def _():
            @pl.when(v + 1 < visits)
            def _():
                add_tiles(v + 1, 0, slots)

        return carry

    lax.fori_loop(0, visits, visit, 0)

    @pl.when(has_outer)
    def _():
        loop(visits * chunks - lead, visits * chunks, step)

    @pl.when(jnp.logical_not(has_outer))
    def _():
        loop(0, chunks - group, lambda k: settle(visits - 1, k, False))

    for j in range(item_tiles):
        panel_copy(visits - 1, j, home).wait_recv()
        panel_out[j * tile:(j + 1) * tile] = vp[visits, j, :width].T

    @pl.when(has_outer)
    def _():
        loop(visits * chunks, visits * chunks + lag, step)

    @pl.when(jnp.logical_not(has_outer))
    def _():
        loop(chunks - group, chunks, lambda k: settle(visits - 1, k, False))

    for j in range(item_tiles):
        loop(0, visits, lambda v: panel_copy(v, j, back).wait_send())
    loop(0, chunks, lambda k: fold_copy(k).wait_send())

    @pl.when(has_outer)
    def _():
        loop(0, chunks, lambda k: user_copy(k).wait_send())


def finish(users, panel, user_out, panel_out, sent):
    copies = [
        pltpu.make_async_copy(users, user_out, sent.at[0]), pltpu.make_async_copy(panel, panel_out, sent.at[1])]
    for copy in copies:
        copy.start()
    for copy in copies:
        copy.wait()


def per_device(
    n_blk, n_split,
    ratings, user_tile, item_tile, tile_count, user_count, item_count, user_factors, item_factors
):
    visits, slots, tile = ratings.shape[1], ratings.shape[3], ratings.shape[-1]
    users, width = user_factors.shape
    part = item_factors.shape[0]
    user_tiles, item_tiles = users // tile, part // tile
    cell_total = user_tiles * item_tiles
    f32 = jnp.float32
    vmem = pl.BlockSpec(memory_space=pltpu.VMEM)
    hbm = pl.BlockSpec(memory_space=pl.ANY)

    lanes = pl.cdiv(slots + cell_total, LANES) * LANES
    held = pl.cdiv(visits, PAD) * PAD
    ch = tile // 2
    chunks = users // ch
    user_gain = step_gain * users / (slots * tile * tile * n_split)
    item_gain = step_gain * part / (slots * tile * tile)
    group, lag, lead, slow = 2, 4, 3, 7
    sizes = (visits, n_blk, n_split, ch, group, lag, lead, slow, user_gain, item_gain)
    dma = pltpu.SemaphoreType.DMA
    shapes = [jax.ShapeDtypeStruct((users, width), f32), jax.ShapeDtypeStruct((part, width), f32)]
    results = pl.pallas_call(
        functools.partial(run_visits, sizes),
        out_shape=[pltpu.VMEM(x.shape, x.dtype) for x in shapes],
        in_specs=[hbm] * 8,
        out_specs=[vmem, vmem],
        scratch_shapes=[
            pltpu.VMEM((users, width), f32),
            pltpu.VMEM((users, width), f32),
            pltpu.VMEM((users, width), f32),
            pltpu.VMEM((users, width), f32),
            pltpu.VMEM((2, users, width), f32),
            pltpu.VMEM((visits + 1, item_tiles, width + PAD, tile), f32),
            pltpu.VMEM((part, width), jnp.bfloat16),
            pltpu.VMEM((width, part), jnp.bfloat16),
            pltpu.VMEM((width, part), f32),
            pltpu.VMEM((2, slots, tile, tile), ratings.dtype),
            pltpu.VMEM((slots + 1, tile, tile), f32),
            pltpu.VMEM((held, lanes), jnp.int32),
            pltpu.VMEM((held, lanes), jnp.int32),
            pltpu.VMEM((held, lanes), f32),
            pltpu.SMEM((held, lanes), jnp.int32),
            pltpu.SMEM((held, lanes), f32),
            pltpu.VMEM((part, width), f32),
            pltpu.SMEM((visits,), jnp.int32),
            pltpu.VMEM((visits, 1, slots), jnp.int32),
            pltpu.VMEM((visits, 1, slots), jnp.int32),
            pltpu.VMEM((users // tile, tile), jnp.int32),
            pltpu.VMEM((item_tiles, tile), jnp.int32),
            dma((chunks,)), dma((chunks,)), dma((2, chunks)), dma((chunks,)), dma((chunks,)),
            dma((visits, item_tiles)), dma((visits, item_tiles)), dma((2, PIECES)), dma((2,)),
            dma((7,)),
        ],
        compiler_params=pltpu.CompilerParams(collective_id=0, has_side_effects=True, vmem_limit_bytes=VMEM_LIMIT),
        name="run_visits",
    )(
        tile_count.reshape(visits), user_tile.reshape(visits, 1, slots), item_tile.reshape(visits, 1, slots),
        ratings.reshape(visits, slots, tile, tile),
        user_count.reshape(users // tile, tile), item_count.reshape(item_tiles, tile), user_factors, item_factors,
    )
    return pl.pallas_call(
        finish, out_shape=shapes, in_specs=[vmem, vmem], out_specs=[hbm, hbm],
        scratch_shapes=[dma((2,))], name="finish",
    )(*(pltpu.with_memory_space_constraint(x, pltpu.VMEM) for x in results))


def solution(mesh):
    return jax.shard_map(
        functools.partial(per_device, mesh.shape["blk"], mesh.shape["split"]),
        mesh=mesh,
        in_specs=(
            P("blk", None, "split", None, None, None),
            P("blk", None, "split", None),
            P("blk", None, "split", None),
            P("blk", None, "split"),
            P("blk"),
            P(("blk", "split")),
            P("blk", None),
            P(("blk", "split"), None),
        ),
        out_specs=(P("blk", None), P(("blk", "split"), None)),
        check_vma=False,
    )
```

```python
import functools

import jax
import jax.numpy as jnp
from jax import lax
from jax.experimental import pallas as pl
from jax.experimental.pallas import tpu as pltpu
from jax.sharding import PartitionSpec as P

MESH = pl.DeviceIdType.MESH
step_gain = 12.0
decay_rate = 0.05
PAD = 8
LANES = 128
PIECES = 4
VMEM_LIMIT = 60 << 20


def column(row, width):
    return jnp.broadcast_to(row, (width, row.shape[1])).T


def run_visits(
    sizes, tile_count_in, user_tile_in, item_tile_in, ratings, user_count_in, item_count_in, user_in, panel_in,
    user_out, panel_out,
    u, ustep, g, fold, peer, vp, v16, v16t, gi, tiles, sums, key, chain_v, live_v, chain, live, turn_v,
    tile_count, user_tile, item_tile, user_count, item_count,
    g_sent, fold_got, peer_got, u_sent, u_got, v_sent, v_got, tiles_got, chain_got, in_got,
):
    visits, n_blk, n_split, ch, group, lag, lead, slow, user_gain, item_gain = sizes
    slots, tile = ratings.shape[1], ratings.shape[-1]
    users, width = user_in.shape
    part = panel_in.shape[0]
    item_tiles = part // tile
    chunks = users // ch
    rows_of = group * ch // tile
    cells_of = rows_of * item_tiles
    f32, bf16 = jnp.float32, jnp.bfloat16

    b, s = lax.axis_index("blk"), lax.axis_index("split")
    half = n_split // 2
    left_side = s < half
    inward = jnp.where(left_side, s + 1, s - 1)
    outward = jnp.where(left_side, s - 1, s + 1)
    middle = (s == half - 1) | (s == half)
    has_outer = (s > 0) & (s < n_split - 1)
    back = lax.rem(b + n_blk - 1, n_blk)
    front = lax.rem(b + 1, n_blk)
    home = lax.rem(b + visits - 1, n_blk)
    guest = lax.rem(b + n_blk * visits - (visits - 1), n_blk)

    barrier = pltpu.get_barrier_semaphore()
    for other in (back, front):
        pl.semaphore_signal(barrier, inc=1, device_id={"blk": other}, device_id_type=MESH)
    pl.semaphore_signal(barrier, inc=1, device_id={"split": inward}, device_id_type=MESH)

    @pl.when(has_outer)
    def _():
        pl.semaphore_signal(barrier, inc=1, device_id={"split": outward}, device_id_type=MESH)

    def rows(k):
        return pl.ds(pl.multiple_of(k * ch, ch), ch)

    def tiles_copy(v, i):
        slot, of = lax.rem(v, 2), pl.ds(i * slots // PIECES, (i + 1) * slots // PIECES - i * slots // PIECES)
        return pltpu.make_async_copy(ratings.at[v, of], tiles.at[slot, of], tiles_got.at[slot, i])

    def start_tiles(v):
        for i in range(PIECES):
            tiles_copy(v, i).start()

    def add_tiles(v, lo, hi):
        slot = lax.rem(v, 2)

        def add(t, carry):
            sums[t + 1] = tiles[slot, t].astype(f32) + sums[chain[v, t]]
            return carry

        lax.fori_loop(lo, hi, add, 0)

    def fold_copy(k):
        return pltpu.make_async_remote_copy(
            src_ref=g.at[rows(k)], dst_ref=fold.at[rows(k)], send_sem=g_sent.at[k],
            recv_sem=fold_got.at[k], device_id={"split": inward}, device_id_type=MESH)

    def peer_copy(v, k):
        par = lax.rem(v, 2)
        return pltpu.make_async_remote_copy(
            src_ref=g.at[rows(k)], dst_ref=peer.at[par, rows(k)], send_sem=g_sent.at[k],
            recv_sem=peer_got.at[par, k], device_id={"split": inward}, device_id_type=MESH)

    def user_copy(k):
        return pltpu.make_async_remote_copy(
            src_ref=u.at[rows(k)], dst_ref=u.at[rows(k)], send_sem=u_sent.at[k],
            recv_sem=u_got.at[k], device_id={"split": outward}, device_id_type=MESH)

    def panel_copy(v, j, to):
        return pltpu.make_async_remote_copy(
            src_ref=vp.at[v, j], dst_ref=vp.at[v + 1, j], send_sem=v_sent.at[v, j],
            recv_sem=v_got.at[v, j], device_id={"blk": to}, device_id_type=MESH)

    pairs = (
        (tile_count_in, tile_count), (user_tile_in, user_tile), (item_tile_in, item_tile),
        (item_count_in, item_count), (user_count_in, user_count), (panel_in, turn_v), (user_in, u))
    in_copies = [pltpu.make_async_copy(a, to, in_got.at[i]) for i, (a, to) in enumerate(pairs)]
    for copy in in_copies:
        copy.start()
    start_tiles(0)
    if visits > 1:
        start_tiles(1)
    cell_total = users // tile * item_tiles
    lane = lax.broadcasted_iota(jnp.int32, key.shape, 1)
    key[...] = lane - slots
    for copy in in_copies[:3]:
        copy.wait()
    at = lax.broadcasted_iota(jnp.int32, (1, slots), 1)
    for v in range(visits):
        cell = user_tile[v] * item_tiles + item_tile[v]
        key[v:v + 1, :slots] = jnp.where(at < tile_count[v], cell, cell_total)
    turned = key[...].T
    chain_v[...] = jnp.zeros_like(chain_v)
    live_v[...] = jnp.zeros_like(live_v)
    number = lax.broadcasted_iota(jnp.int32, (slots, key.shape[1]), 0)
    ahead = lax.broadcasted_iota(jnp.int32, number.shape, 1)
    ahead = jnp.minimum(ahead, slots)
    for v in range(visits):
        same = turned[:slots, v:v + 1] == key[v:v + 1]
        chain_v[v:v + 1] = jnp.max(
            jnp.where(same & (number < ahead), number + 1, 0), axis=0, keepdims=True)
        live_v[v:v + 1] = jnp.sum(jnp.where(same, 1.0, 0.0), axis=0, keepdims=True)
    chain_copies = [
        pltpu.make_async_copy(chain_v, chain, chain_got.at[0]), pltpu.make_async_copy(live_v, live, chain_got.at[1])]
    for copy in chain_copies:
        copy.start()
    sums[0] = jnp.zeros(sums.shape[1:], f32)
    for copy in in_copies[3:6]:
        copy.wait()
    item_step = item_gain / jnp.sqrt(item_count[...].astype(f32))
    user_step = user_gain / jnp.sqrt(user_count[...].astype(f32))
    for a in range(users // tile):
        ustep[a * tile:(a + 1) * tile] = column(user_step[a:a + 1], width)
    for j in range(item_tiles):
        vp[0, j, :width] = turn_v[j * tile:(j + 1) * tile].T
        vp[0, j, width:] = jnp.broadcast_to(item_step[j:j + 1], (PAD, tile))
    for copy in chain_copies:
        copy.wait()
    for i in range(PIECES):
        tiles_copy(0, i).wait()
        add_tiles(0, i * slots // PIECES, (i + 1) * slots // PIECES)
    in_copies[6].wait()
    pl.semaphore_wait(barrier, jnp.where(has_outer, 4, 3))

    def grads(v, q):
        of = pl.ds(pl.multiple_of(q * group * ch, group * ch), group * ch)
        user_half = u[of].astype(bf16)
        predicted = jnp.dot(user_half, v16t[...], preferred_element_type=f32)
        high, low = [], []
        for a in range(rows_of):
            hs, ls = [], []
            for j in range(item_tiles):
                c = q * cells_of + a * item_tiles + j
                err = sums[chain[v, slots + c]] - live[v, slots + c] * predicted[
                    a * tile:(a + 1) * tile, j * tile:(j + 1) * tile]
                h = err.astype(bf16)
                hs.append(h)
                ls.append((err - h.astype(f32)).astype(bf16))
            high.append(jnp.concatenate(hs, axis=1))
            low.append(jnp.concatenate(ls, axis=1))
        both = jnp.concatenate(high + low, axis=0)
        gu = jnp.dot(both, v16[...], preferred_element_type=f32)
        gu = gu[:group * ch] + gu[group * ch:]
        @pl.when(v > 0)
        def _():
            for k in range(group):
                fold_copy(q * group + k).wait_send()

        g[of] = gu

        @pl.when(jnp.logical_not(has_outer))
        def _():
            for k in range(group):
                send_in(v, q * group + k, False)

        over = (((0,), (0,)), ((), ()))
        twice = jnp.concatenate([user_half, user_half], axis=0)
        gi[...] += lax.dot_general(twice, both, over, preferred_element_type=f32)

    def send_in(v, k, inner):
        @choose(middle, known_middle(inner))
        def _():
            peer_copy(v, k).start()

        @choose(jnp.logical_not(middle), negated(known_middle(inner)))
        def _():
            fold_copy(k).start()

    def known_middle(inner):
        return inner if n_split == 4 else None

    def negated(known):
        return None if known is None else not known

    def choose(cond, known):
        def run(body):
            if known is None:
                pl.when(cond)(body)
            elif known:
                body()

        return run

    def pass_in(v, k):
        fold_copy(k).wait_recv()
        g[rows(k)] += fold[rows(k)]
        send_in(v, k, True)

    def settle(v, k, inner):
        if inner:
            @pl.when(v > 0)
            def _():
                user_copy(k).wait_send()

        @choose(middle, known_middle(inner))
        def _():
            peer_copy(v, k).wait_recv()
            old = u[rows(k)]
            grad = g[rows(k)] + peer[lax.rem(v, 2), rows(k)]
            u[rows(k)] = old + ustep[rows(k)] * (grad - decay_rate * old)

        @choose(jnp.logical_not(middle), negated(known_middle(inner)))
        def _():
            user_copy(k).wait_recv()

        if inner:
            user_copy(k).start()

        @pl.when(v == visits - 1)
        def _():
            user_out[rows(k)] = u[rows(k)]

    def loop(lo, hi, step):
        def body(k, carry):
            step(k)
            return carry

        lax.fori_loop(lo, hi, body, 0)

    groups = chunks // group
    turned = 2 * (groups - 1) - slow
    rest = chunks - turned

    def step(i):
        @pl.when(i >= 0)
        def _():
            pass_in(i // chunks, i % chunks)

        @pl.when(i >= lag)
        def _():
            settle((i - lag) // chunks, (i - lag) % chunks, True)

    def visit(v, carry):
        gi[...] = jnp.zeros_like(gi)
        for j in range(item_tiles):
            @pl.when(v > 0)
            def _():
                panel_copy(v - 1, j, back).wait_recv()

            at = slice(j * tile, (j + 1) * tile)
            items = vp[v, j, :width]
            v16t[:, at] = items.astype(bf16)
            v16[at] = items.astype(bf16).T

        def turn(q):
            @pl.when(jnp.logical_not(has_outer) & (v > 0))
            def _():
                for k in range(group):
                    settle(v - 1, q * group + k, False)

            grads(v, q)

            @pl.when(has_outer & (q < groups - 1))
            def _():
                at = v * chunks - lead + q + jnp.maximum(q - slow, 0)
                step(at)

                @pl.when(q >= slow)
                def _():
                    step(at + 1)

        loop(0, groups, turn)
        for j in range(item_tiles):
            at = slice(j * tile, (j + 1) * tile)
            old = vp[v, j, :width]
            vp[v, j, :width] = old + vp[v, j, width:width + 1] * (gi[:, at] - decay_rate * old)

            @pl.when(v < visits - 1)
            def _():
                panel_copy(v, j, back).start()

            @pl.when(v == visits - 1)
            def _():
                panel_copy(v, j, home).start()

        @pl.when(v + 1 < visits)
        def _():
            for i in range(PIECES):
                tiles_copy(v + 1, i).wait()

        @pl.when(v + 2 < visits)
        def _():
            start_tiles(v + 2)

        @pl.when(has_outer)
        def _():
            def early(k):
                pass_in(v, turned - lead + k)
                settle(v, turned - lead - lag + k, True)

                @pl.when(v + 1 < visits)
                def _():
                    add_tiles(v + 1, k * slots // rest, (k + 1) * slots // rest)

            loop(0, rest, early)

        @pl.when(jnp.logical_not(has_outer))
        def _():
            @pl.when(v + 1 < visits)
            def _():
                add_tiles(v + 1, 0, slots)

        return carry

    lax.fori_loop(0, visits, visit, 0)

    @pl.when(has_outer)
    def _():
        loop(visits * chunks - lead, visits * chunks, step)

    @pl.when(jnp.logical_not(has_outer))
    def _():
        loop(0, chunks - group, lambda k: settle(visits - 1, k, False))

    for j in range(item_tiles):
        panel_copy(visits - 1, j, home).wait_recv()
        panel_out[j * tile:(j + 1) * tile] = vp[visits, j, :width].T

    @pl.when(has_outer)
    def _():
        loop(chunks - lag, chunks, lambda k: settle(visits - 1, k, True))

    @pl.when(jnp.logical_not(has_outer))
    def _():
        loop(chunks - group, chunks, lambda k: settle(visits - 1, k, False))

    for j in range(item_tiles):
        loop(0, visits, lambda v: panel_copy(v, j, back).wait_send())
    loop(0, chunks, lambda k: fold_copy(k).wait_send())

    @pl.when(has_outer)
    def _():
        loop(0, chunks, lambda k: user_copy(k).wait_send())


def finish(users, panel, user_out, panel_out, sent):
    copies = [
        pltpu.make_async_copy(users, user_out, sent.at[0]), pltpu.make_async_copy(panel, panel_out, sent.at[1])]
    for copy in copies:
        copy.start()
    for copy in copies:
        copy.wait()


def per_device(
    n_blk, n_split,
    ratings, user_tile, item_tile, tile_count, user_count, item_count, user_factors, item_factors
):
    visits, slots, tile = ratings.shape[1], ratings.shape[3], ratings.shape[-1]
    users, width = user_factors.shape
    part = item_factors.shape[0]
    user_tiles, item_tiles = users // tile, part // tile
    cell_total = user_tiles * item_tiles
    f32 = jnp.float32
    vmem = pl.BlockSpec(memory_space=pltpu.VMEM)
    hbm = pl.BlockSpec(memory_space=pl.ANY)

    lanes = pl.cdiv(slots + cell_total, LANES) * LANES
    held = pl.cdiv(visits, PAD) * PAD
    ch = tile // 2
    chunks = users // ch
    user_gain = step_gain * users / (slots * tile * tile * n_split)
    item_gain = step_gain * part / (slots * tile * tile)
    group, lag, lead, slow = 2, 4, 3, 7
    sizes = (visits, n_blk, n_split, ch, group, lag, lead, slow, user_gain, item_gain)
    dma = pltpu.SemaphoreType.DMA
    shapes = [jax.ShapeDtypeStruct((users, width), f32), jax.ShapeDtypeStruct((part, width), f32)]
    results = pl.pallas_call(
        functools.partial(run_visits, sizes),
        out_shape=[pltpu.VMEM(x.shape, x.dtype) for x in shapes],
        in_specs=[hbm] * 8,
        out_specs=[vmem, vmem],
        scratch_shapes=[
            pltpu.VMEM((users, width), f32),
            pltpu.VMEM((users, width), f32),
            pltpu.VMEM((users, width), f32),
            pltpu.VMEM((users, width), f32),
            pltpu.VMEM((2, users, width), f32),
            pltpu.VMEM((visits + 1, item_tiles, width + PAD, tile), f32),
            pltpu.VMEM((part, width), jnp.bfloat16),
            pltpu.VMEM((width, part), jnp.bfloat16),
            pltpu.VMEM((width, part), f32),
            pltpu.VMEM((2, slots, tile, tile), ratings.dtype),
            pltpu.VMEM((slots + 1, tile, tile), f32),
            pltpu.VMEM((held, lanes), jnp.int32),
            pltpu.VMEM((held, lanes), jnp.int32),
            pltpu.VMEM((held, lanes), f32),
            pltpu.SMEM((held, lanes), jnp.int32),
            pltpu.SMEM((held, lanes), f32),
            pltpu.VMEM((part, width), f32),
            pltpu.SMEM((visits,), jnp.int32),
            pltpu.VMEM((visits, 1, slots), jnp.int32),
            pltpu.VMEM((visits, 1, slots), jnp.int32),
            pltpu.VMEM((users // tile, tile), jnp.int32),
            pltpu.VMEM((item_tiles, tile), jnp.int32),
            dma((chunks,)), dma((chunks,)), dma((2, chunks)), dma((chunks,)), dma((chunks,)),
            dma((visits, item_tiles)), dma((visits, item_tiles)), dma((2, PIECES)), dma((2,)),
            dma((7,)),
        ],
        compiler_params=pltpu.CompilerParams(collective_id=0, has_side_effects=True, vmem_limit_bytes=VMEM_LIMIT),
        name="run_visits",
    )(
        tile_count.reshape(visits), user_tile.reshape(visits, 1, slots), item_tile.reshape(visits, 1, slots),
        ratings.reshape(visits, slots, tile, tile),
        user_count.reshape(users // tile, tile), item_count.reshape(item_tiles, tile), user_factors, item_factors,
    )
    return pl.pallas_call(
        finish, out_shape=shapes, in_specs=[vmem, vmem], out_specs=[hbm, hbm],
        scratch_shapes=[dma((2,))], name="finish",
    )(*(pltpu.with_memory_space_constraint(x, pltpu.VMEM) for x in results))


def solution(mesh):
    return jax.shard_map(
        functools.partial(per_device, mesh.shape["blk"], mesh.shape["split"]),
        mesh=mesh,
        in_specs=(
            P("blk", None, "split", None, None, None),
            P("blk", None, "split", None),
            P("blk", None, "split", None),
            P("blk", None, "split"),
            P("blk"),
            P(("blk", "split")),
            P("blk", None),
            P(("blk", "split"), None),
        ),
        out_specs=(P("blk", None), P(("blk", "split"), None)),
        check_vma=False,
    )
```
